256 devices in a mesh: req: 32 (over z, y_hi, core), tp: 8 (over y_lo, x).
Axes of the slice: x: 4, y: 4 (y_hi: 2, y_lo: 2; y = y_hi * 2 + y_lo), z: 8, core: 2. Of those that a mesh axis runs over, the one named last changes fastest.
Arguments:
- tokens: bfloat16 [32768, 1024], P(('req', 'tp')), may hold values from -1.5 to 1.5
- segment_ids: int32 [32768], replicated, may hold values from 0 to 3, never falling along the last dimension, each value on 1 to 16384 neighbouring positions
- variate_ids: int32 [32768], replicated, may hold values from 0 to 7
- time_ids: int32 [32768], P('req'), may hold values from 0 to 511
- attn_gain: float32 [1024], replicated, may hold values from 0.25 to 1.75
- q_weight: bfloat16 [1024, 1024], P(None, 'tp'), may hold values from -0.1875 to 0.1875
- k_weight: bfloat16 [1024, 1024], P(None, 'tp'), may hold values from -0.1875 to 0.1875
- v_weight: bfloat16 [1024, 1024], P(None, 'tp'), may hold values from -0.1875 to 0.1875
- out_weight: bfloat16 [1024, 1024], P('tp'), may hold values from -0.75 to 0.75
- var_bias: float32 [2, 16], P(None, 'tp'), may hold values from -3 to 253
- ffn_gain: float32 [1024], replicated, may hold values from 0.25 to 1.75
- gate_weight: bfloat16 [1024, 4096], P(None, 'tp'), may hold values from -0.1875 to 0.1875
- up_weight: bfloat16 [1024, 4096], P(None, 'tp'), may hold values from -0.1875 to 0.1875
- down_weight: bfloat16 [4096, 1024], P('tp'), may hold values from -0.09375 to 0.09375
Outputs:
- layer_out: bfloat16 [32768, 1024], P(('req', 'tp'))
The draws below stay inside these ranges and needn't reach their ends.
Inputs may be any that keep to these rules, and one draw needn't show every extreme that they name: `segment_ids`: never falling along the pack; each prompt holds at most 16384 tokens and one holds exactly 16384.
All inputs are finite; a program needn't handle non-finite values.
Results may differ from the reference program's by a relative error of at most 0.015.
Values may be sent and summed in bfloat16 or wider, within the bound.
No kernel may reach another device: no remote copies, remote signals or barrier semaphores. Data moves between devices by JAX's collectives and lax.ppermute only.
A program may use at most 64 MiB of HBM per device.

```python
import math
import jax
import jax.numpy as jnp
import numpy as np
from jax import lax

HEADS = 16
HEAD_DIM = 64
FF = 4096
TOK_DEV = 1024
VARS = 8
TIME_RANGE = 512
SEGS = 4
D = 1024
TOKENS = 32768
LONGEST = 16384


def draw_var_bias(key, part):
    first_key = jax.random.fold_in(jax.random.fold_in(key, 7), 0)
    base = jax.random.uniform(first_key, (2, HEADS), jnp.float32, -3.0, 3.0)
    return base


def plant(drawn, own_key, smallest, top_value):
    spot = [jax.random.randint(jax.random.fold_in(own_key, axis), (), 0, length) for axis, length in enumerate(drawn.shape)]
    widest = drawn.shape.index(max(drawn.shape))
    neighbour = spot[:widest] + [(spot[widest] + 1) % drawn.shape[widest]] + spot[widest + 1:]
    return drawn.at[tuple(spot)].set(smallest).at[tuple(neighbour)].set(top_value)


def steps_of(rng, shape, cuts, least, high):
    def one(position, parts):
        steps = jax.random.uniform(jax.random.fold_in(jax.random.fold_in(rng, 6), position), (parts,), jnp.float32, least / len(cuts), high / len(cuts))
        return jnp.repeat(jnp.exp(steps), shape[position] // parts).reshape((-1,) + (1,) * (len(shape) - position - 1))

    level = one(*cuts[0])
    for cut in cuts[1:]:
        level = level * one(*cut)
    return level


def split_up(amount, total, most, lean):
    weights = [(1 << 20) // math.isqrt(rank ** lean) + 1 for rank in range(2, amount + 1)]
    spare, counts = total - most - (amount - 1), [1] * (amount - 1)
    while spare > 0:
        free = [i for i in range(amount - 1) if counts[i] < most]
        whole, remaining = sum([weights[i] for i in free]), spare
        for i in free:
            addition = min(most - counts[i], max(1, remaining * weights[i] // whole), spare)
            counts[i] = counts[i] + addition
            spare = spare - addition
    return np.array([most] + counts)


def ragged(key, amount, total, limit, skew):
    if amount == 2:
        one = jax.random.randint(key, (), max(1, total - limit), min(limit, total - 1) + 1)
        return jnp.stack([one, total - one])
    sizes = jnp.asarray(split_up(amount, total, limit, skew), jnp.int32)
    couples = (amount - 1) // 2
    source_of, receiver = sizes[1:1 + 2 * couples:2], sizes[2:2 + 2 * couples:2]
    margin = jnp.minimum(source_of - 1, limit - receiver)
    moved = jax.random.randint(jax.random.fold_in(key, 1), (couples,), 0, 1 << 20) % (margin + 1)
    sizes = sizes.at[1:1 + 2 * couples:2].set(source_of - moved).at[2:2 + 2 * couples:2].set(receiver + moved)
    return sizes[jax.random.permutation(jax.random.fold_in(key, 2), amount)]


def bell_draw(key, dims, deviation, bound, shards=(), kind=jnp.bfloat16):
    values = deviation * jax.random.normal(key, dims, jnp.float32)
    if shards:
        values = values * steps_of(key, dims, shards, -0.22, 0.18)
    return jnp.clip(values, -bound, bound).astype(kind)


def setup_inputs(seed: int = 0) -> dict:
    seeds = jax.random.split(jax.random.key(seed), 15)
    return {
        "tokens": bell_draw(seeds[0], (TOKENS, D), 0.25, 1.5, ((0, 256),)),
        "segment_ids": jnp.searchsorted(jnp.cumsum(ragged(seeds[1], SEGS, TOKENS, LONGEST, 2)), jnp.arange(TOKENS), side="right").astype(jnp.int32),
        "variate_ids": plant(jax.random.randint(seeds[2], (TOKENS,), 0, VARS), jax.random.fold_in(seeds[2], 1), 0, VARS - 1).astype(jnp.int32),
        "time_ids": plant(jax.random.randint(seeds[3], (TOKENS,), 0, TIME_RANGE), jax.random.fold_in(seeds[3], 1), 0, TIME_RANGE - 1).astype(jnp.int32),
        "attn_gain": jnp.clip(1.0 + 0.15 * jax.random.normal(seeds[4], (D,), jnp.float32), 0.25, 1.75),
        "q_weight": bell_draw(seeds[5], (D, D), D ** -0.5, 0.1875, ((1, 8),)),
        "k_weight": bell_draw(seeds[6], (D, D), D ** -0.5, 0.1875, ((1, 8),)),
        "v_weight": bell_draw(seeds[7], (D, D), D ** -0.5, 0.1875, ((1, 8),)),
        "out_weight": bell_draw(seeds[8], (D, D), (D // 16) ** -0.5, 0.75, ((0, 8),)),
        "var_bias": draw_var_bias(jax.random.fold_in(seeds[14], 71), 0),
        "ffn_gain": jnp.clip(1.0 + 0.15 * jax.random.normal(seeds[10], (D,), jnp.float32), 0.25, 1.75),
        "gate_weight": bell_draw(seeds[11], (D, FF), D ** -0.5, 0.1875, ((1, 8),)),
        "up_weight": bell_draw(seeds[12], (D, FF), D ** -0.5, 0.1875, ((1, 8),)),
        "down_weight": bell_draw(seeds[13], (FF, D), FF ** -0.5, 0.09375, ((0, 8),)),
    }


big_negative = -1e+30

def norm_rows(rows, gain):
    values = rows.astype(jnp.float32)
    scale = lax.rsqrt(lax.optimization_barrier(jnp.mean(values * values, axis=-1, keepdims=True)) + 1e-05)
    return values * scale * gain.astype(jnp.float32)

def rotary(values, times):
    width = values.shape[-1]
    half = width // 2
    freq = 10000.0 ** (-2.0 * jnp.arange(half, dtype=jnp.float32) / width)
    angle = times.astype(jnp.float32)[:, None] * freq[None, :]
    cosine = jnp.cos(angle)[:, None, :]
    sine = jnp.sin(angle)[:, None, :]
    first = values[..., :half]
    second = values[..., half:]
    return jnp.concatenate([first * cosine - second * sine, first * sine + second * cosine], axis=-1)

def project_rows(normed, times, q_weight, k_weight, v_weight, head_dim):
    count = normed.shape[0]
    heads = q_weight.shape[1] // head_dim
    query = jnp.dot(normed, q_weight, preferred_element_type=jnp.float32).reshape(count, heads, head_dim)
    query = (rotary(query, times) * head_dim ** (-0.5)).astype(jnp.bfloat16).reshape(count, -1)
    keys = jnp.dot(normed, k_weight, preferred_element_type=jnp.float32).reshape(count, heads, head_dim)
    keys = rotary(keys, times).astype(jnp.bfloat16).reshape(count, -1)
    values = jnp.dot(normed, v_weight, preferred_element_type=jnp.float32).astype(jnp.bfloat16)
    return jnp.concatenate([query, keys, values], axis=1)

def attend(carry, query, q_seg, q_var, keys, values, k_seg, k_var, var_bias):
    most, total, accum = carry
    scores = jnp.einsum('qhe,khe->hqk', query.astype(jnp.float32), keys.astype(jnp.float32))
    same = (q_var[:, None] == k_var[None, :])[None]
    scores = scores + jnp.where(same, var_bias[0][:, None, None], var_bias[1][:, None, None])
    mask = (q_seg[:, None] == k_seg[None, :])[None]
    top = jnp.maximum(most, lax.optimization_barrier(jnp.max(jnp.where(mask, scores, big_negative), axis=-1)))
    fade = jnp.exp(most - top)
    weights = jnp.where(mask, jnp.exp(scores - top[..., None]), 0.0)
    total = total * fade + lax.optimization_barrier(jnp.sum(weights, axis=-1))
    rounded = weights.astype(jnp.bfloat16).astype(jnp.float32)
    accum = accum * jnp.transpose(fade)[:, :, None] + jnp.einsum('hqk,khe->qhe', rounded, values.astype(jnp.float32))
    return (top, total, accum)

def hidden_units(normed, gate_weight, up_weight):
    gate = jnp.dot(normed, gate_weight, preferred_element_type=jnp.float32)
    upper = jnp.dot(normed, up_weight, preferred_element_type=jnp.float32)
    return (jax.nn.silu(gate) * upper).astype(jnp.bfloat16)

def reference(tokens, segment_ids, variate_ids, time_ids, attn_gain, q_weight, k_weight, v_weight, out_weight, var_bias, ffn_gain, gate_weight, up_weight, down_weight):
    blocks = TOKENS // TOK_DEV
    normed = norm_rows(tokens, attn_gain).astype(jnp.bfloat16)
    packed = project_rows(normed, time_ids, q_weight, k_weight, v_weight, HEAD_DIM)
    query = packed[:, :D].reshape(blocks, TOK_DEV, HEADS, HEAD_DIM)
    keys = packed[:, D:2 * D].reshape(blocks, TOK_DEV, HEADS, HEAD_DIM)
    values = packed[:, 2 * D:].reshape(blocks, TOK_DEV, HEADS, HEAD_DIM)
    seg_blocks = segment_ids.reshape(blocks, TOK_DEV)
    kind_blocks = variate_ids.reshape(blocks, TOK_DEV)
    bias = var_bias.astype(jnp.float32)

    def one_block(inputs):
        block_query, q_seg, q_var = inputs
        start_state = (jnp.full((HEADS, TOK_DEV), big_negative, jnp.float32), jnp.zeros((HEADS, TOK_DEV), jnp.float32), jnp.zeros((TOK_DEV, HEADS, HEAD_DIM), jnp.float32))

        def visit(state, other):
            block_keys, block_values, k_seg, k_var = other
            touch = (k_seg[0] <= q_seg[-1]) & (k_seg[-1] >= q_seg[0])
            result = lax.cond(touch, lambda inner: attend(inner, block_query, q_seg, q_var, block_keys, block_values, k_seg, k_var, bias), lambda inner: inner, state)
            return (result, None)
        final, unused = lax.scan(visit, start_state, (keys, values, seg_blocks, kind_blocks))
        total = final[1]
        accum = final[2]
        return (accum / jnp.transpose(total)[:, :, None]).astype(jnp.bfloat16).reshape(TOK_DEV, D)
    attended = lax.map(one_block, (query, seg_blocks, kind_blocks)).reshape(TOKENS, D)
    resid = tokens.astype(jnp.float32) + jnp.dot(attended, out_weight, preferred_element_type=jnp.float32)
    hidden = hidden_units(norm_rows(resid, ffn_gain).astype(jnp.bfloat16), gate_weight, up_weight)
    return (resid + jnp.dot(hidden, down_weight, preferred_element_type=jnp.float32)).astype(jnp.bfloat16)
```

```python
import functools

import jax
import jax.numpy as jnp
from jax import lax
from jax.experimental import pallas as pl
from jax.experimental.pallas import tpu as pltpu
from jax.sharding import Mesh, PartitionSpec as P

HEAD_DIM = 64
LOG2E = 1.4426950408889634
MASKED = -1e30
UNSEEN = -3e38
LARGEST = 80.0
BLOCK = 1024
KEYS = 2048
ROWS = 512
REQ = ("z", "yh", "c")
TP = ("yl", "x")
PAIR = 2 * BLOCK
PADDED = PAIR + ROWS
BF16 = jnp.bfloat16
HBM = pl.BlockSpec(memory_space=pltpu.HBM)
F32 = jnp.float32


def norm_rows(rows, gain):
    values = rows.astype(F32)
    scale = lax.rsqrt(jnp.mean(values * values, axis=-1, keepdims=True) + 1e-05)
    return values * scale * gain


def gather_rows(rows, axes, count):
    copies = jnp.broadcast_to(rows[None], (count,) + rows.shape)
    return lax.all_to_all(
        copies.reshape((count * rows.shape[0],) + rows.shape[1:]), axes, 0, 0, tiled=True
    )


def project_kernel(yh_ref, *refs):
    sources, results, scratch, outputs, load_sems, store_sems = (
        refs[:6],
        refs[6:9],
        refs[9:15],
        refs[15:19],
        refs[19],
        refs[20],
    )
    step = 256
    x_scr, qw_scr, kw_scr, vw_scr, cos_scr, sin_scr = scratch
    loads = [
        pltpu.make_async_copy(source, target, load_sems.at[i])
        for i, (source, target) in enumerate(zip(sources[1:], scratch[1:]))
    ]
    chunks = [
        pltpu.make_async_copy(
            sources[0].at[pl.ds(i, step)], x_scr.at[pl.ds(i, step)], load_sems.at[5 + i // step]
        )
        for i in range(0, BLOCK, step)
    ]
    for copy in loads + chunks:
        copy.start()
    for copy in loads:
        copy.wait()
    lane = lax.broadcasted_iota(jnp.int32, (step, 128), 1)
    first_half = (lane & 63) < 32
    left = lane < HEAD_DIM
    here_low = jnp.broadcast_to(yh_ref[0], lane.shape) == 0
    dot = functools.partial(jnp.dot, preferred_element_type=F32)
    mine, kv_send, q_send, q_here = outputs
    for i in range(0, BLOCK, step):
        chunks[i // step].wait()
        at = slice(i, i + step)
        x, cosine, sine = x_scr[at, :], cos_scr[at, :], sin_scr[at, :]

        def turn(values):
            partner = jnp.where(
                first_half, -pltpu.roll(values, 96, 1), pltpu.roll(values, 32, 1)
            )
            return values * cosine + partner * sine

        query = turn(dot(x, qw_scr[...])) * (LOG2E * HEAD_DIM**-0.5)
        key = turn(dot(x, kw_scr[...]))
        value = dot(x, vw_scr[...])
        low = jnp.where(left, key, pltpu.roll(value, 64, 1))
        high = jnp.where(left, pltpu.roll(key, 64, 1), value)
        mine[at, :] = jnp.where(here_low, low, high).astype(BF16)
        kv_send[at, :] = jnp.where(here_low, high, low).astype(BF16)
        low = jnp.where(left, query, 0.0)
        high = jnp.where(left, pltpu.roll(query, 64, 1), 0.0)
        q_here[at, :] = jnp.where(here_low, low, high).astype(BF16)
        q_send[at, :] = jnp.where(here_low, high, low).astype(BF16)
    targets = (results[0].at[pl.ds(0, BLOCK)], results[1].at[0], results[1].at[1], results[2])
    stores = [
        pltpu.make_async_copy(output, target, store_sems.at[i])
        for i, (output, target) in enumerate(zip(outputs, targets))
    ]
    for copy in stores:
        copy.start()
    for copy in stores:
        copy.wait()


def project(yh, rows, q_weight, k_weight, v_weight, cosine, sine):
    block = pltpu.VMEM((BLOCK, 128), BF16)
    table = pltpu.VMEM((BLOCK, 128), F32)
    return pl.pallas_call(
        project_kernel,
        out_shape=(
            jax.ShapeDtypeStruct((PAIR, 128), BF16),
            jax.ShapeDtypeStruct((2, BLOCK, 128), BF16),
            jax.ShapeDtypeStruct((BLOCK, 128), BF16),
        ),
        in_specs=[pl.BlockSpec(memory_space=pltpu.SMEM)] + [HBM] * 6,
        out_specs=(HBM,) * 3,
        scratch_shapes=[pltpu.VMEM((BLOCK, 1024), BF16)]
        + [block] * 3
        + [table] * 2
        + [block] * 4
        + [pltpu.SemaphoreType.DMA((9,)), pltpu.SemaphoreType.DMA((4,))],
        compiler_params=pltpu.CompilerParams(vmem_limit_bytes=30 << 20),
        name="project",
    )(
        yh,
        *(
            pltpu.with_memory_space_constraint(array, pltpu.HBM)
            for array in (rows, q_weight, k_weight, v_weight, cosine, sine)
        ),
    )


def hot_rows(variate, segment, shape):
    row = lax.broadcasted_iota(jnp.int32, shape, 0)
    variate = jnp.broadcast_to(variate, shape)
    segment = jnp.broadcast_to(segment, shape)
    return row, jnp.where(row < 24, (row & 7) - variate, row - 24 - segment) == 0


def query_side_kernel(at_ref, bias_ref, variate_ref, segment_ref, out_ref):
    for part in range(PAIR // 128):
        block, offset = divmod(part, 8)
        line = at_ref[block] + offset
        row, hot = hot_rows(
            variate_ref[pl.ds(line, 1), :], segment_ref[pl.ds(line, 1), :], (HEAD_DIM, 128)
        )
        bias = jnp.where(row < 8, bias_ref[0], jnp.where(row < 16, bias_ref[1], bias_ref[2]))
        masked = jnp.where(row < 28, MASKED, 0.0)
        columns = jnp.where(row < 24, jnp.where(hot, bias, 0.0), jnp.where(hot, 0.0, masked))
        both = jnp.concatenate([jnp.zeros((HEAD_DIM, 128), F32), columns], axis=0)
        out_ref[part * 128 : (part + 1) * 128, :] = both.T.astype(BF16)
    lane = lax.broadcasted_iota(jnp.int32, (PADDED - PAIR, 128), 1)
    out_ref[PAIR:, :] = jnp.where((lane >= 88) & (lane < 92), MASKED, 0.0).astype(BF16)


def query_side(at, bias, variates, segments):
    smem = pl.BlockSpec(memory_space=pltpu.SMEM)
    vmem = pl.BlockSpec(memory_space=pltpu.VMEM)
    return pl.pallas_call(
        query_side_kernel,
        out_shape=jax.ShapeDtypeStruct((PADDED, 128), BF16),
        in_specs=[smem, smem, vmem, vmem],
        out_specs=vmem,
        name="query_side",
    )(at, bias, variates, segments)


def attend_kernel(place_ref, which_ref, start_ref, count_ref, bias_ref, raised_in, *refs, groups, first):
    extra_ref, variate_ref, segment_ref, here_ref, there_ref, sums_in, top_in = refs[:7]
    kv_refs, rest = refs[7 : 7 + 2 * groups], refs[7 + 2 * groups :]
    sums_out, top_out, raised_out, sums_scr, top_scr, pair_scr, query_scr, kv_scr, key_scr, value_scr, state_sem, kv_sem = rest
    loads = [pltpu.make_async_copy(ref, kv_scr.at[i], kv_sem.at[i]) for i, ref in enumerate(kv_refs)]
    query_loads = [
        pltpu.make_async_copy(here_ref, pair_scr.at[0], kv_sem.at[2 * groups]),
        pltpu.make_async_copy(there_ref.at[1], pair_scr.at[1], kv_sem.at[2 * groups + 1]),
    ]
    for load in query_loads + loads:
        load.start()
    if first:
        sums_scr[...] = jnp.zeros_like(sums_scr)
    else:
        state_load = pltpu.make_async_copy(sums_in, sums_scr, state_sem)
        state_load.start()
    yh, core = place_ref[0], place_ref[1]
    largest = 0.0
    for number, row in enumerate((yh, 1 - yh)):
        query_loads[number].wait()
        at = pl.ds(pl.multiple_of(row * BLOCK, BLOCK), BLOCK)
        value = pair_scr[number]
        query_scr[at, :] = value + extra_ref[at, :]
        value = value.astype(F32)
        largest = jnp.maximum(largest, jnp.max(jnp.sum(value * value, axis=1)))
    query_scr[PAIR:, :] = extra_ref[PAIR:, :]
    raised_out[0] = raised_in[0]
    allowed = LARGEST - jnp.abs(bias_ref[0])

    for load in loads:
        load.wait()
    def prepare(number, carry):
        name = which_ref[number]

        @pl.when(count_ref[name] > 0)
        def _():
            rows = pl.ds(pl.multiple_of(number % 2 * BLOCK, BLOCK), BLOCK)
            longest = jnp.zeros((1, BLOCK), F32)
            for half in range(2):
                kv = kv_scr[number // 2 * 2 + half, rows, :]
                at = slice(half * BLOCK, (half + 1) * BLOCK)
                lane = lax.broadcasted_iota(jnp.int32, kv.shape, 1)
                value_scr[number, at, :] = jnp.where(lane >= HEAD_DIM, kv, jnp.ones_like(kv))
                keys = kv.T[:HEAD_DIM, :]
                key_scr[number, :HEAD_DIM, at] = keys
                keys = keys.astype(F32)
                longest = jnp.maximum(longest, jnp.sum(keys * keys, axis=0, keepdims=True))
                block = name * 2 + (core if half == 0 else 1 - core)
                for part in range(8):
                    line = pl.ds(block * 8 + part, 1)
                    _, hot = hot_rows(variate_ref[line, :], segment_ref[line, :], (HEAD_DIM, 128))
                    column = half * BLOCK + part * 128
                    key_scr[number, HEAD_DIM:, column : column + 128] = jnp.where(
                        hot, 1.0, 0.0
                    ).astype(BF16)
            within = (allowed > 0) & (1.01 * largest * jnp.max(longest) <= allowed * allowed)
            raised_out[0] = jnp.where(within, raised_out[0], 1)

        return carry

    lax.fori_loop(0, 2 * groups, prepare, 0)
    if not first:
        state_load.wait()
    raised = raised_out[0]

    @pl.when(raised == 0)
    def _():
        def tile(number, carry):
            start = start_ref[which_ref[number]]

            def visit(index, inner):
                at = pl.ds(pl.multiple_of(start + index * ROWS, 64), ROWS)
                scores = jnp.dot(query_scr[at, :], key_scr[number], preferred_element_type=F32)
                weights = jnp.exp2(scores).astype(BF16)
                sums_scr[at, :] += jnp.dot(weights, value_scr[number], preferred_element_type=F32)
                return inner

            return lax.fori_loop(0, count_ref[which_ref[number]], visit, carry)

        lax.fori_loop(0, 2 * groups, tile, 0)

    @pl.when(raised != 0)
    def _():
        pltpu.sync_copy(top_in, top_scr)

        def tile(number, carry):
            start = start_ref[which_ref[number]]

            def visit(index, inner):
                at = pl.ds(pl.multiple_of(start + index * 256, 64), 256)
                query = query_scr[at, :]

                def part(piece, deep):
                    columns = pl.ds(pl.multiple_of(piece * 256, 256), 256)
                    scores = jnp.dot(
                        query, key_scr[number, :, columns], preferred_element_type=F32
                    )
                    sums = sums_scr[at, :]
                    old = jnp.where(sums[:, :1] > 0, top_scr[at, :], UNSEEN)
                    new = jnp.maximum(old, jnp.max(scores, axis=1, keepdims=True))
                    weights = jnp.exp2(scores - new[:, :1]).astype(BF16)
                    sums_scr[at, :] = sums * jnp.exp2(old - new) + jnp.dot(
                        weights, value_scr[number, columns, :], preferred_element_type=F32
                    )
                    top_scr[at, :] = new
                    return deep

                return lax.fori_loop(0, KEYS // 256, part, inner)

            return lax.fori_loop(0, count_ref[which_ref[number]] * (ROWS // 256), visit, carry)

        lax.fori_loop(0, 2 * groups, tile, 0)
        pltpu.sync_copy(top_scr, top_out)

    pltpu.sync_copy(sums_scr, sums_out)


def attend(place, which, start, count, bias, queries, ids, keys_values, state, first):
    groups = len(keys_values) // 2
    sums, top, raised = state
    smem = pl.BlockSpec(memory_space=pltpu.SMEM)
    vmem = pl.BlockSpec(memory_space=pltpu.VMEM)
    shape = jax.ShapeDtypeStruct((PADDED, 128), F32)
    stay = lambda arrays: tuple(pltpu.with_memory_space_constraint(a, pltpu.HBM) for a in arrays)
    operands = (queries[2],) + ids + stay(queries[:2] + (sums, top)) + tuple(keys_values)
    return pl.pallas_call(
        functools.partial(attend_kernel, groups=groups, first=first),
        out_shape=(shape, shape, jax.ShapeDtypeStruct((1,), jnp.int32)),
        in_specs=[smem] * 6 + [vmem] * 3 + [HBM] * (4 + len(keys_values)),
        out_specs=(HBM, HBM, smem),
        input_output_aliases={11: 0, 12: 1},
        scratch_shapes=[
            pltpu.VMEM((PADDED, 128), F32),
            pltpu.VMEM((PADDED, 128), F32),
            pltpu.VMEM((2, BLOCK, 128), BF16),
            pltpu.VMEM((PADDED, 128), BF16),
            pltpu.VMEM((2 * groups, PAIR, 128), BF16),
            pltpu.VMEM((2 * groups, 128, KEYS), BF16),
            pltpu.VMEM((2 * groups, KEYS, 128), BF16),
            pltpu.SemaphoreType.DMA,
            pltpu.SemaphoreType.DMA((2 * groups + 2,)),
        ],
        compiler_params=pltpu.CompilerParams(vmem_limit_bytes=40 << 20),
        name="attend",
    )(place, which, start, count, bias, raised, *operands)


def out_kernel(parts_ref, weight_ref, tokens_ref, gain_ref, resid_ref, ffn_in_ref, rows_scr):
    left = lax.broadcasted_iota(jnp.int32, (64, 128), 1) < HEAD_DIM
    for t in range(8):
        low, high = parts_ref[t].astype(F32), parts_ref[8 + t].astype(F32)
        at = slice(t * 128, (t + 1) * 128)
        rows_scr[:64, at] = jnp.where(left, low, pltpu.roll(high, 64, 1)).astype(BF16)
        rows_scr[64:, at] = jnp.where(left, pltpu.roll(low, 64, 1), high).astype(BF16)
    resid = tokens_ref[...].astype(F32) + jnp.dot(
        rows_scr[...], weight_ref[...], preferred_element_type=F32
    )
    resid_ref[...] = resid
    ffn_in_ref[...] = norm_rows(resid, gain_ref[...]).astype(BF16)


def out_projection(parts, weight, tokens, gain):
    vmem = pl.BlockSpec(memory_space=pltpu.VMEM)
    return pl.pallas_call(
        out_kernel,
        out_shape=(
            jax.ShapeDtypeStruct(tokens.shape, F32),
            jax.ShapeDtypeStruct(tokens.shape, BF16),
        ),
        in_specs=[vmem] * 4,
        out_specs=(vmem, vmem),
        scratch_shapes=[pltpu.VMEM(tokens.shape, BF16)],
        name="out_projection",
    )(parts, weight, tokens, gain.reshape(1, -1))


def ffn_kernel(near_ref, away_ref, shared, own_ref, far_ref, shared_scr, sems):
    copies = [
        pltpu.make_async_copy(shared.at[i], shared_scr.at[i], sems.at[i])
        for i in range(shared.shape[0])
    ]
    for copy in copies:
        copy.start()
    dot = functools.partial(jnp.dot, preferred_element_type=F32)
    x = jnp.concatenate([near_ref[...], away_ref[...]], axis=0)
    total = None
    for low in range(0, len(copies), 2):
        copies[low].wait()
        copies[low + 1].wait()
        both = dot(x[:, :512], shared_scr[low, :512, :])
        both = both + dot(x[:, 512:], shared_scr[low + 1, :512, :])
        hidden = (jax.nn.silu(both[:, :512]) * both[:, 512:]).astype(BF16)
        part = dot(hidden[:, :256], shared_scr[low, 512:, :])
        part = part + dot(hidden[:, 256:], shared_scr[low + 1, 512:, :])
        total = part if total is None else total + part
    half = total.shape[0] // 2
    own_ref[...] = total[:half]
    far_ref[...] = total[half:].astype(BF16)


def feed_forward(near, away, shared):
    rows, width = near.shape
    vmem = pl.BlockSpec(memory_space=pltpu.VMEM)
    return pl.pallas_call(
        ffn_kernel,
        out_shape=(
            jax.ShapeDtypeStruct((rows, width), F32),
            jax.ShapeDtypeStruct((rows, width), BF16),
        ),
        in_specs=[vmem, vmem, HBM],
        out_specs=(vmem, vmem),
        scratch_shapes=[
            pltpu.VMEM(shared.shape, BF16),
            pltpu.SemaphoreType.DMA((shared.shape[0],)),
        ],
        compiler_params=pltpu.CompilerParams(vmem_limit_bytes=40 << 20),
        name="feed_forward",
    )(near, away, pltpu.with_memory_space_constraint(shared, pltpu.HBM))


def per_device(
    tokens,
    segment_ids,
    variate_ids,
    time_ids,
    attn_gain,
    q_weight,
    k_weight,
    v_weight,
    out_weight,
    var_bias,
    ffn_gain,
    gate_weight,
    up_weight,
    down_weight,
):
    z, yh, c = lax.axis_index("z"), lax.axis_index("yh"), lax.axis_index("c")
    pick = functools.partial(lax.dynamic_index_in_dim, keepdims=False)

    with jax.named_scope("gather_normed"):
        normed = norm_rows(tokens, attn_gain).astype(BF16)
        rows = gather_rows(normed, TP, 8)

    with jax.named_scope("tables"):
        lane = lax.broadcasted_iota(jnp.int32, (1, 128), 1)
        freq = 10000.0 ** (-2.0 * (lane & 31).astype(F32) / HEAD_DIM)
        angle = time_ids.astype(F32)[:, None] * freq
        cosine, sine = jnp.cos(angle), jnp.sin(angle)
        bias = pick(var_bias, yh, 1)
        rest = rest_bias = (bias[0] - bias[1]) * LOG2E
        pieces = []
        for _ in range(3):
            piece = lax.reduce_precision(rest, 8, 7)
            pieces.append(piece)
            rest = rest - piece
        number = lambda *values: jnp.stack(values).astype(jnp.int32)
        segments = segment_ids.reshape(256, 128)
        variates = variate_ids.reshape(256, 128)
        at = number(z * 32 + c * 8, z * 32 + 16 + c * 8)
        extra = query_side(at, jnp.stack(pieces), variates, segments)
        blocks = segment_ids.reshape(8, 2, 2, BLOCK)
        q_seg = pick(pick(blocks, z, 0), c, 1).reshape(1, PAIR)
        low_seg = segments[::16, :1]
        high_seg = segments[15::16, 127:]
        begin = jnp.sum((q_seg < low_seg).astype(jnp.int32), axis=1)
        end = jnp.sum((q_seg <= high_seg).astype(jnp.int32), axis=1)
        start = begin // 64 * 64
        count = jnp.where(end > begin, (end - start + ROWS - 1) // ROWS, 0)
        take = lax.dynamic_slice_in_dim
        pack = jnp.concatenate(
            [
                jnp.concatenate(
                    [take(gate_weight, c * 512, 512), take(up_weight, c * 512, 512)], axis=1
                ),
                take(down_weight, c * 256, 256),
            ],
            axis=0,
        )
        rows, cosine, sine, extra, start, count, pack = lax.optimization_barrier(
            (rows, cosine, sine, extra, start, count, pack)
        )

    swap = [(0, 1), (1, 0)]
    with jax.named_scope("project"):
        mine, send, q_here = project(
            number(yh), rows, q_weight, k_weight, v_weight, cosine, sine
        )

    with jax.named_scope("exchange"):
        there = lax.ppermute(send, "yh", swap)
        mine = lax.dynamic_update_slice_in_dim(mine, there[0], BLOCK, axis=0)
        ahead = [(i, (i - 1) % 8) for i in range(8)]
        behind = [(i, (i + 1) % 8) for i in range(8)]

    with jax.named_scope("share_weights"):
        rows, out_part = lax.optimization_barrier((rows, out_weight))
        out_full = lax.all_gather(out_part, TP, axis=0, tiled=True)
        shared = lax.all_gather(pack, ("x", "c"), axis=0, tiled=True).reshape(8, 768, 1024)

    with jax.named_scope("attention"):
        place = number(yh, c)
        zeros = jnp.zeros((PADDED, 128), F32)
        state = (zeros, zeros + 0.0, jnp.zeros((1,), jnp.int32))
        gap = rest_bias.reshape(1)
        up, down = mine, mine
        parts = [mine]
        for hop, steps in enumerate(((0,), (1, 7), (2, 6), (3, 5, 4))):
            others = [lax.ppermute(part, "c", swap) for part in parts]
            which = number(
                *((z + k) % 8 * 2 + side for k in steps for side in (yh, 1 - yh))
            )
            if hop < 3:
                up = lax.ppermute(up, "z", ahead)
                down = lax.ppermute(down, "z", behind)
            state = attend(
                place,
                which,
                start,
                count,
                gap,
                (q_here, there, extra),
                (variates, segments),
                [part for pair in zip(parts, others) for part in pair],
                state,
                hop == 0,
            )
            parts = [up, down]
            if hop == 0:
                state, distant = lax.optimization_barrier((state, mine))
                distant = lax.ppermute(distant, "z", [(i, (i - 4) % 8) for i in range(8)])
            if hop == 2:
                parts = [up, down, distant]
            state, parts = lax.optimization_barrier((tuple(state), parts))
            up, down = parts[:2]
        sums = state[0]
        sums, shared = lax.optimization_barrier((sums, shared))

    with jax.named_scope("to_rows"):
        attended = (sums[:PAIR, HEAD_DIM:] / sums[:PAIR, :1]).astype(BF16)
        attended = attended.reshape(16, 2, 64, HEAD_DIM)
        attended = jnp.concatenate([attended[:, 0], attended[:, 1]], axis=-1)
        attended = lax.all_to_all(attended, ("yh", "yl", "x"), 0, 0, tiled=True)

    with jax.named_scope("out_projection"):
        resid, ffn_in = out_projection(attended, out_full, tokens, ffn_gain)

    with jax.named_scope("feed_forward"):
        own, far = feed_forward(ffn_in, lax.ppermute(ffn_in, "yl", swap), shared)
        back = lax.ppermute(far, "yl", swap)
        return (resid + (own + back.astype(F32))).astype(BF16)


def solution(mesh):
    split = Mesh(mesh.devices.reshape(8, 2, 2, 2, 4), ("z", "yh", "c", "yl", "x"))
    return jax.shard_map(
        per_device,
        mesh=split,
        in_specs=(
            P(REQ + TP, None),
            P(),
            P(),
            P(REQ),
            P(),
            P(None, TP),
            P(None, TP),
            P(None, TP),
            P(TP, None),
            P(None, TP),
            P(),
            P(None, TP),
            P(None, TP),
            P(TP, None),
        ),
        out_specs=P(REQ + TP, None),
        check_vma=False,
    )
```

```python
import functools

import jax
import jax.numpy as jnp
from jax import lax
from jax.experimental import pallas as pl
from jax.experimental.pallas import tpu as pltpu
from jax.sharding import Mesh, PartitionSpec as P

HEAD_DIM = 64
LOG2E = 1.4426950408889634
MASKED = -1e30
UNSEEN = -3e38
LARGEST = 80.0
BLOCK = 1024
KEYS = 2048
ROWS = 512
REQ = ("z", "yh", "c")
TP = ("yl", "x")
UNITS = 768
PAIR = 2 * BLOCK
PADDED = PAIR + ROWS
BF16 = jnp.bfloat16
HBM = pl.BlockSpec(memory_space=pltpu.HBM)
F32 = jnp.float32


def norm_rows(rows, gain):
    values = rows.astype(F32)
    scale = lax.rsqrt(jnp.mean(values * values, axis=-1, keepdims=True) + 1e-05)
    return values * scale * gain


def gather_rows(rows, axes, count):
    copies = jnp.broadcast_to(rows[None], (count,) + rows.shape)
    return lax.all_to_all(
        copies.reshape((count * rows.shape[0],) + rows.shape[1:]), axes, 0, 0, tiled=True
    )


def project_kernel(yh_ref, *refs):
    sources, results, scratch, outputs, load_sems, store_sems = (
        refs[:6],
        refs[6:9],
        refs[9:15],
        refs[15:19],
        refs[19],
        refs[20],
    )
    step = 256
    x_scr, qw_scr, kw_scr, vw_scr, cos_scr, sin_scr = scratch
    loads = [
        pltpu.make_async_copy(source, target, load_sems.at[i])
        for i, (source, target) in enumerate(zip(sources[1:], scratch[1:]))
    ]
    chunks = [
        pltpu.make_async_copy(
            sources[0].at[pl.ds(i, step)], x_scr.at[pl.ds(i, step)], load_sems.at[5 + i // step]
        )
        for i in range(0, BLOCK, step)
    ]
    for copy in loads + chunks:
        copy.start()
    for copy in loads:
        copy.wait()
    lane = lax.broadcasted_iota(jnp.int32, (step, 128), 1)
    first_half = (lane & 63) < 32
    left = lane < HEAD_DIM
    here_low = jnp.broadcast_to(yh_ref[0], lane.shape) == 0
    dot = functools.partial(jnp.dot, preferred_element_type=F32)
    mine, kv_send, q_send, q_here = outputs
    sent = []
    for i in range(0, BLOCK, step):
        chunks[i // step].wait()
        at = slice(i, i + step)
        x, cosine, sine = x_scr[at, :], cos_scr[at, :], sin_scr[at, :]

        def turn(values):
            partner = jnp.where(
                first_half, -pltpu.roll(values, 96, 1), pltpu.roll(values, 32, 1)
            )
            return values * cosine + partner * sine

        query = turn(dot(x, qw_scr[...])) * (LOG2E * HEAD_DIM**-0.5)
        key = turn(dot(x, kw_scr[...]))
        value = dot(x, vw_scr[...])
        low = jnp.where(left, key, pltpu.roll(value, 64, 1))
        high = jnp.where(left, pltpu.roll(key, 64, 1), value)
        mine[at, :] = jnp.where(here_low, low, high).astype(BF16)
        kv_send[at, :] = jnp.where(here_low, high, low).astype(BF16)
        low = jnp.where(left, query, 0.0)
        high = jnp.where(left, pltpu.roll(query, 64, 1), 0.0)
        q_here[at, :] = jnp.where(here_low, low, high).astype(BF16)
        sent.append(jnp.where(here_low, high, low))
        if i >= BLOCK // 2:
            both = jnp.where(left, sent[i // step - 2], pltpu.roll(sent[i // step], 64, 1))
            q_send[i - BLOCK // 2 : i - BLOCK // 2 + step, :] = both.astype(BF16)
    targets = (
        results[0].at[pl.ds(0, BLOCK)],
        results[1].at[pl.ds(0, BLOCK)],
        results[1].at[pl.ds(BLOCK, BLOCK // 2)],
        results[2],
    )
    stores = [
        pltpu.make_async_copy(output, target, store_sems.at[i])
        for i, (output, target) in enumerate(zip(outputs, targets))
    ]
    for copy in stores:
        copy.start()
    for copy in stores:
        copy.wait()


def project(yh, rows, q_weight, k_weight, v_weight, cosine, sine):
    block = pltpu.VMEM((BLOCK, 128), BF16)
    table = pltpu.VMEM((BLOCK, 128), F32)
    return pl.pallas_call(
        project_kernel,
        out_shape=(
            pltpu.HBM((PAIR, 128), BF16),
            jax.ShapeDtypeStruct((BLOCK + BLOCK // 2, 128), BF16),
            pltpu.HBM((BLOCK, 128), BF16),
        ),
        in_specs=[pl.BlockSpec(memory_space=pltpu.SMEM)] + [HBM] * 6,
        out_specs=(HBM,) * 3,
        scratch_shapes=[pltpu.VMEM((BLOCK, 1024), BF16)]
        + [block] * 3
        + [table] * 2
        + [block, block, pltpu.VMEM((BLOCK // 2, 128), BF16), block]
        + [pltpu.SemaphoreType.DMA((9,)), pltpu.SemaphoreType.DMA((4,))],
        compiler_params=pltpu.CompilerParams(vmem_limit_bytes=30 << 20),
        name="project",
    )(
        yh,
        *(
            pltpu.with_memory_space_constraint(array, pltpu.HBM)
            for array in (rows, q_weight, k_weight, v_weight, cosine, sine)
        ),
    )


def hot_rows(variate, segment, shape):
    row = lax.broadcasted_iota(jnp.int32, shape, 0)
    variate = jnp.broadcast_to(variate, shape)
    segment = jnp.broadcast_to(segment, shape)
    return row, jnp.where(row < 24, (row & 7) - variate, row - 24 - segment) == 0


def query_side_kernel(at_ref, bias_ref, variate_ref, segment_ref, out_ref):
    for part in range(PAIR // 128):
        block, offset = divmod(part, 8)
        line = at_ref[block] + offset
        row, hot = hot_rows(
            variate_ref[pl.ds(line, 1), :], segment_ref[pl.ds(line, 1), :], (HEAD_DIM, 128)
        )
        bias = jnp.where(row < 8, bias_ref[0], jnp.where(row < 16, bias_ref[1], bias_ref[2]))
        masked = jnp.where(row < 28, MASKED, 0.0)
        columns = jnp.where(row < 24, jnp.where(hot, bias, 0.0), jnp.where(hot, 0.0, masked))
        both = jnp.concatenate([jnp.zeros((HEAD_DIM, 128), F32), columns], axis=0)
        out_ref[part * 128 : (part + 1) * 128, :] = both.T.astype(BF16)
    lane = lax.broadcasted_iota(jnp.int32, (PADDED - PAIR, 128), 1)
    out_ref[PAIR:, :] = jnp.where((lane >= 88) & (lane < 92), MASKED, 0.0).astype(BF16)


def query_side(at, bias, variates, segments):
    smem = pl.BlockSpec(memory_space=pltpu.SMEM)
    vmem = pl.BlockSpec(memory_space=pltpu.VMEM)
    return pl.pallas_call(
        query_side_kernel,
        out_shape=jax.ShapeDtypeStruct((PADDED, 128), BF16),
        in_specs=[smem, smem, vmem, vmem],
        out_specs=vmem,
        name="query_side",
    )(at, bias, variates, segments)


def attend_kernel(
    place_ref, which_ref, start_ref, count_ref, bias_ref, raised_in, *refs, groups, first, last
):
    extra_ref, variate_ref, segment_ref, here_ref, there_ref = refs[:5]
    refs = refs[5:]
    if not first:
        (sums_in, top_in), refs = refs[:2], refs[2:]
    kv_refs, refs = refs[: 2 * groups], refs[2 * groups :]
    if last:
        attended_ref, refs = refs[0], refs[1:]
    else:
        (sums_out, top_out, raised_out), refs = refs[:3], refs[3:]
    (
        sums_scr,
        top_scr,
        near_scr,
        away_scr,
        query_scr,
        kv_scr,
        key_scr,
        value_scr,
        raised_scr,
        state_sem,
        kv_sem,
    ) = refs
    loads = [pltpu.make_async_copy(ref, kv_scr.at[i], kv_sem.at[i]) for i, ref in enumerate(kv_refs)]
    query_loads = [
        pltpu.make_async_copy(here_ref, near_scr, kv_sem.at[2 * groups]),
        pltpu.make_async_copy(
            there_ref.at[pl.ds(BLOCK, BLOCK // 2)], away_scr, kv_sem.at[2 * groups + 1]
        ),
    ]
    for load in query_loads + loads:
        load.start()
    if first:
        sums_scr[...] = jnp.zeros_like(sums_scr)
    else:
        state_load = pltpu.make_async_copy(sums_in, sums_scr, state_sem)
        state_load.start()
    yh, core = place_ref[0], place_ref[1]
    largest = 0.0
    for load in query_loads:
        load.wait()
    left = lax.broadcasted_iota(jnp.int32, (BLOCK // 2, 128), 1) < HEAD_DIM
    near, away = near_scr[...].astype(F32), away_scr[...].astype(F32)
    for row, value in (
        (yh * 2, near[: BLOCK // 2]),
        (yh * 2 + 1, near[BLOCK // 2 :]),
        ((1 - yh) * 2, jnp.where(left, away, 0.0)),
        ((1 - yh) * 2 + 1, jnp.where(left, pltpu.roll(away, 64, 1), 0.0)),
    ):
        at = pl.ds(pl.multiple_of(row * (BLOCK // 2), BLOCK // 2), BLOCK // 2)
        query_scr[at, :] = value.astype(BF16) + extra_ref[at, :]
        largest = jnp.maximum(largest, jnp.max(jnp.sum(value * value, axis=1)))
    query_scr[PAIR:, :] = extra_ref[PAIR:, :]
    raised_scr[0] = raised_in[0]
    allowed = LARGEST - jnp.abs(bias_ref[0])

    for load in loads:
        load.wait()
    def prepare(number, carry):
        name = which_ref[number]

        @pl.when(count_ref[name] > 0)
        def _():
            rows = pl.ds(pl.multiple_of(number % 2 * BLOCK, BLOCK), BLOCK)
            longest = jnp.zeros((1, BLOCK), F32)
            for half in range(2):
                kv = kv_scr[number // 2 * 2 + half, rows, :]
                at = slice(half * BLOCK, (half + 1) * BLOCK)
                lane = lax.broadcasted_iota(jnp.int32, kv.shape, 1)
                value_scr[number, at, :] = jnp.where(lane >= HEAD_DIM, kv, jnp.ones_like(kv))
                keys = kv.T[:HEAD_DIM, :]
                key_scr[number, :HEAD_DIM, at] = keys
                keys = keys.astype(F32)
                longest = jnp.maximum(longest, jnp.sum(keys * keys, axis=0, keepdims=True))
                block = name * 2 + (core if half == 0 else 1 - core)
                for part in range(8):
                    line = pl.ds(block * 8 + part, 1)
                    _, hot = hot_rows(variate_ref[line, :], segment_ref[line, :], (HEAD_DIM, 128))
                    column = half * BLOCK + part * 128
                    key_scr[number, HEAD_DIM:, column : column + 128] = jnp.where(
                        hot, 1.0, 0.0
                    ).astype(BF16)
            within = (allowed > 0) & (1.01 * largest * jnp.max(longest) <= allowed * allowed)
            raised_scr[0] = jnp.where(within, raised_scr[0], 1)

        return carry

    lax.fori_loop(0, 2 * groups, prepare, 0)
    if not first:
        state_load.wait()
    raised = raised_scr[0]
    if not last:
        raised_out[0] = raised

    @pl.when(raised == 0)
    def _():
        def tile(number, carry):
            start = start_ref[which_ref[number]]

            def visit(index, inner):
                at = pl.ds(pl.multiple_of(start + index * ROWS, 64), ROWS)
                scores = jnp.dot(query_scr[at, :], key_scr[number], preferred_element_type=F32)
                weights = jnp.exp2(scores).astype(BF16)
                sums_scr[at, :] += jnp.dot(weights, value_scr[number], preferred_element_type=F32)
                return inner

            return lax.fori_loop(0, count_ref[which_ref[number]], visit, carry)

        lax.fori_loop(0, 2 * groups, tile, 0)

    @pl.when(raised != 0)
    def _():
        top_scr[...] = jnp.zeros_like(top_scr)
        if not first:

            @pl.when(raised_in[0] != 0)
            def _():
                pltpu.sync_copy(top_in, top_scr)

        def tile(number, carry):
            start = start_ref[which_ref[number]]

            def visit(index, inner):
                at = pl.ds(pl.multiple_of(start + index * 256, 64), 256)
                query = query_scr[at, :]

                def part(piece, deep):
                    columns = pl.ds(pl.multiple_of(piece * 256, 256), 256)
                    scores = jnp.dot(
                        query, key_scr[number, :, columns], preferred_element_type=F32
                    )
                    sums = sums_scr[at, :]
                    old = jnp.where(sums[:, :1] > 0, top_scr[at, :], UNSEEN)
                    new = jnp.maximum(old, jnp.max(scores, axis=1, keepdims=True))
                    weights = jnp.exp2(scores - new[:, :1]).astype(BF16)
                    sums_scr[at, :] = sums * jnp.exp2(old - new) + jnp.dot(
                        weights, value_scr[number, columns, :], preferred_element_type=F32
                    )
                    top_scr[at, :] = new
                    return deep

                return lax.fori_loop(0, KEYS // 256, part, inner)

            return lax.fori_loop(0, count_ref[which_ref[number]] * (ROWS // 256), visit, carry)

        lax.fori_loop(0, 2 * groups, tile, 0)
        if not last:
            pltpu.sync_copy(top_scr, top_out)

    if not last:
        pltpu.sync_copy(sums_scr, sums_out)
        return
    left = lax.broadcasted_iota(jnp.int32, (64, 128), 1) < HEAD_DIM
    for part in range(PAIR // 128):
        one = sums_scr[part * 128 : part * 128 + 64, :]
        two = sums_scr[part * 128 + 64 : part * 128 + 128, :]
        value = jnp.where(left, pltpu.roll(one, 64, 1), two)
        total = jnp.where(left, one, pltpu.roll(two, 64, 1))
        attended_ref[part] = (value / total).astype(BF16)


def attend(place, which, start, count, bias, queries, ids, keys_values, state, last):
    groups = len(keys_values) // 2
    first = state is None
    smem = pl.BlockSpec(memory_space=pltpu.SMEM)
    vmem = pl.BlockSpec(memory_space=pltpu.VMEM)
    stay = lambda arrays: tuple(pltpu.with_memory_space_constraint(a, pltpu.HBM) for a in arrays)
    held = queries[:2] + (() if first else state[:2])
    operands = (queries[2],) + ids + stay(held) + tuple(keys_values)
    raised = jnp.zeros((1,), jnp.int32) if first else state[2]
    shape = pltpu.HBM((PADDED, 128), F32)
    if last:
        out_shape, out_specs = jax.ShapeDtypeStruct((16, 64, 128), BF16), vmem
    else:
        out_shape = (shape, shape, jax.ShapeDtypeStruct((1,), jnp.int32))
        out_specs = (HBM, HBM, smem)
    return pl.pallas_call(
        functools.partial(attend_kernel, groups=groups, first=first, last=last),
        out_shape=out_shape,
        in_specs=[smem] * 6 + [vmem] * 3 + [HBM] * (len(operands) - 3),
        out_specs=out_specs,
        input_output_aliases={} if first or last else {11: 0, 12: 1},
        scratch_shapes=[
            pltpu.VMEM((PADDED, 128), F32),
            pltpu.VMEM((PADDED, 128), F32),
            pltpu.VMEM((BLOCK, 128), BF16),
            pltpu.VMEM((BLOCK // 2, 128), BF16),
            pltpu.VMEM((PADDED, 128), BF16),
            pltpu.VMEM((2 * groups, PAIR, 128), BF16),
            pltpu.VMEM((2 * groups, 128, KEYS), BF16),
            pltpu.VMEM((2 * groups, KEYS, 128), BF16),
            pltpu.SMEM((1,), jnp.int32),
            pltpu.SemaphoreType.DMA,
            pltpu.SemaphoreType.DMA((2 * groups + 2,)),
        ],
        compiler_params=pltpu.CompilerParams(vmem_limit_bytes=44 << 20),
        name="attend",
    )(place, which, start, count, bias, raised, *operands)


def out_kernel(parts_ref, weight_ref, tokens_ref, gain_ref, resid_ref, ffn_in_ref, rows_scr):
    left = lax.broadcasted_iota(jnp.int32, (64, 128), 1) < HEAD_DIM
    for t in range(8):
        low, high = parts_ref[t].astype(F32), parts_ref[8 + t].astype(F32)
        at = slice(t * 128, (t + 1) * 128)
        rows_scr[:64, at] = jnp.where(left, low, pltpu.roll(high, 64, 1)).astype(BF16)
        rows_scr[64:, at] = jnp.where(left, pltpu.roll(low, 64, 1), high).astype(BF16)
    resid = tokens_ref[...].astype(F32) + jnp.dot(
        rows_scr[...], weight_ref[...], preferred_element_type=F32
    )
    resid_ref[...] = resid
    ffn_in_ref[...] = norm_rows(resid, gain_ref[...]).astype(BF16)


def out_projection(parts, weight, tokens, gain):
    vmem = pl.BlockSpec(memory_space=pltpu.VMEM)
    return pl.pallas_call(
        out_kernel,
        out_shape=(
            jax.ShapeDtypeStruct(tokens.shape, F32),
            jax.ShapeDtypeStruct(tokens.shape, BF16),
        ),
        in_specs=[vmem] * 4,
        out_specs=(vmem, vmem),
        scratch_shapes=[pltpu.VMEM(tokens.shape, BF16)],
        name="out_projection",
    )(parts, weight, tokens, gain.reshape(1, -1))


def ffn_kernel(near_ref, away_ref, shared, own_ref, far_ref, shared_scr, sems):
    copies = [
        pltpu.make_async_copy(shared.at[i, pl.ds(0, UNITS)], shared_scr.at[i], sems.at[i])
        for i in range(shared.shape[0])
    ]
    for copy in copies:
        copy.start()
    dot = functools.partial(jnp.dot, preferred_element_type=F32)
    x = jnp.concatenate([near_ref[...], away_ref[...]], axis=0)
    total = None
    for low in range(0, len(copies), 2):
        copies[low].wait()
        copies[low + 1].wait()
        both = dot(x[:, :512], shared_scr[low, :512, :])
        both = both + dot(x[:, 512:], shared_scr[low + 1, :512, :])
        hidden = (jax.nn.silu(both[:, :512]) * both[:, 512:]).astype(BF16)
        part = dot(hidden[:, :256], shared_scr[low, 512:UNITS, :])
        part = part + dot(hidden[:, 256:], shared_scr[low + 1, 512:UNITS, :])
        total = part if total is None else total + part
    half = total.shape[0] // 2
    own_ref[...] = total[:half]
    far_ref[...] = total[half:].astype(BF16)


def feed_forward(near, away, shared):
    rows, width = near.shape
    vmem = pl.BlockSpec(memory_space=pltpu.VMEM)
    return pl.pallas_call(
        ffn_kernel,
        out_shape=(
            jax.ShapeDtypeStruct((rows, width), F32),
            jax.ShapeDtypeStruct((rows, width), BF16),
        ),
        in_specs=[vmem, vmem, HBM],
        out_specs=(vmem, vmem),
        scratch_shapes=[
            pltpu.VMEM((8, UNITS, 1024), BF16),
            pltpu.SemaphoreType.DMA((8,)),
        ],
        compiler_params=pltpu.CompilerParams(vmem_limit_bytes=40 << 20),
        name="feed_forward",
    )(near, away, pltpu.with_memory_space_constraint(shared, pltpu.HBM))


def per_device(
    tokens,
    segment_ids,
    variate_ids,
    time_ids,
    attn_gain,
    q_weight,
    k_weight,
    v_weight,
    out_weight,
    var_bias,
    ffn_gain,
    gate_weight,
    up_weight,
    down_weight,
):
    z, yh, c = lax.axis_index("z"), lax.axis_index("yh"), lax.axis_index("c")
    pick = functools.partial(lax.dynamic_index_in_dim, keepdims=False)

    swap = [(0, 1), (1, 0)]
    number = lambda *values: jnp.stack(values).astype(jnp.int32)
    lane = lax.broadcasted_iota(jnp.int32, (1, 128), 1)

    with jax.named_scope("gather_normed"):
        normed = norm_rows(tokens, attn_gain).astype(BF16)
        rows = gather_rows(normed, TP, 8)

    with jax.named_scope("tables"):
        freq = 10000.0 ** (-2.0 * (lane & 31).astype(F32) / HEAD_DIM)
        angle = time_ids.astype(F32)[:, None] * freq
        cosine, sine = jnp.cos(angle), jnp.sin(angle)
        bias = pick(var_bias, yh, 1)
        rest = rest_bias = (bias[0] - bias[1]) * LOG2E
        pieces = []
        for _ in range(3):
            piece = lax.reduce_precision(rest, 8, 7)
            pieces.append(piece)
            rest = rest - piece
        take = lax.dynamic_slice_in_dim
        segments = segment_ids.reshape(256, 128)
        variates = variate_ids.reshape(256, 128)
        at = number(z * 32 + c * 8, z * 32 + 16 + c * 8)
        extra = query_side(at, jnp.stack(pieces), variates, segments)
        blocks = segment_ids.reshape(8, 2, 2, BLOCK)
        q_seg = pick(pick(blocks, z, 0), c, 1).reshape(1, PAIR)
        low_seg = segments[::16, :1]
        high_seg = segments[15::16, 127:]
        begin = jnp.sum((q_seg < low_seg).astype(jnp.int32), axis=1)
        end = jnp.sum((q_seg <= high_seg).astype(jnp.int32), axis=1)
        start = begin // 64 * 64
        count = jnp.where(end > begin, (end - start + ROWS - 1) // ROWS, 0)
        pack = jnp.concatenate(
            [
                jnp.concatenate(
                    [take(gate_weight, c * 512, 512), take(up_weight, c * 512, 512)], axis=1
                ),
                take(down_weight, c * 256, 256),
            ],
            axis=0,
        )
        rows, cosine, sine, extra, start, count, pack = lax.optimization_barrier(
            (rows, cosine, sine, extra, start, count, pack)
        )

    with jax.named_scope("share_weights"):
        shared = lax.all_gather(pack, ("x", "c"), axis=0, tiled=True).reshape(8, UNITS, 1024)

    with jax.named_scope("project"):
        mine, send, q_here = project(
            number(yh), rows, q_weight, k_weight, v_weight, cosine, sine
        )

    with jax.named_scope("exchange"):
        there = lax.ppermute(send, "yh", swap)
        there, out_part = lax.optimization_barrier((there, out_weight))
        out_full = lax.all_gather(out_part, TP, axis=0, tiled=True)
        mine = lax.dynamic_update_slice_in_dim(mine, there[:BLOCK], BLOCK, axis=0)

    with jax.named_scope("attention"):
        ahead = lambda array, k: lax.ppermute(array, "z", [(i, (i - k) % 8) for i in range(8)])
        place = number(yh, c)
        gap = rest_bias.reshape(1)
        state = None
        parts = [mine]
        hops = ((0,), (1, 7), (2, 6), (3, 5), (4,))
        for hop, steps in enumerate(hops):
            others = [lax.ppermute(part, "c", swap) for part in parts]
            which = number(
                *((z + k) % 8 * 2 + side for k in steps for side in (yh, 1 - yh))
            )
            coming = [ahead(parts[0], 1)] if hop < 4 else []
            if hop < 3:
                coming.append(ahead(parts[-1], -1))
            state = attend(
                place,
                which,
                start,
                count,
                gap,
                (q_here, there, extra),
                (variates, segments),
                [part for pair in zip(parts, others) for part in pair],
                state,
                hop == 4,
            )
            if hop < 4:
                state, parts = lax.optimization_barrier((state, coming))
        state, shared, out_full = lax.optimization_barrier((state, shared, out_full))

    with jax.named_scope("to_rows"):
        attended = lax.all_to_all(state, ("yh", "yl", "x"), 0, 0, tiled=True)

    with jax.named_scope("out_projection"):
        resid, ffn_in = out_projection(attended, out_full, tokens, ffn_gain)

    with jax.named_scope("feed_forward"):
        own, far = feed_forward(ffn_in, lax.ppermute(ffn_in, "yl", swap), shared)
        back = lax.ppermute(far, "yl", swap)
        return (resid + (own + back.astype(F32))).astype(BF16)


def solution(mesh):
    split = Mesh(mesh.devices.reshape(8, 2, 2, 2, 4), ("z", "yh", "c", "yl", "x"))
    return jax.shard_map(
        per_device,
        mesh=split,
        in_specs=(
            P(REQ + TP, None),
            P(),
            P(),
            P(REQ),
            P(),
            P(None, TP),
            P(None, TP),
            P(None, TP),
            P(TP, None),
            P(None, TP),
            P(),
            P(None, TP),
            P(None, TP),
            P(TP, None),
        ),
        out_specs=P(REQ + TP, None),
        check_vma=False,
    )
```

```python
import functools

import jax
import jax.numpy as jnp
from jax import lax
from jax.experimental import pallas as pl
from jax.experimental.pallas import tpu as pltpu
from jax.sharding import Mesh, PartitionSpec as P

HEAD_DIM = 64
LOG2E = 1.4426950408889634
MASKED = -1e30
UNSEEN = -3e38
LARGEST = 80.0
BLOCK = 1024
KEYS = 2048
ROWS = 512
REQ = ("z", "yh", "c")
TP = ("yl", "x")
UNITS = 768
PAIR = 2 * BLOCK
PADDED = PAIR + ROWS
BF16 = jnp.bfloat16
HBM = pl.BlockSpec(memory_space=pltpu.HBM)
F32 = jnp.float32


def norm_rows(rows, gain):
    values = rows.astype(F32)
    scale = lax.rsqrt(jnp.mean(values * values, axis=-1, keepdims=True) + 1e-05)
    return values * scale * gain


def gather_rows(rows, axes, count):
    copies = jnp.broadcast_to(rows[None], (count,) + rows.shape)
    return lax.all_to_all(
        copies.reshape((count * rows.shape[0],) + rows.shape[1:]), axes, 0, 0, tiled=True
    )


def project_kernel(yh_ref, *refs):
    sources, results, scratch, outputs, load_sems, store_sems = (
        refs[:6],
        refs[6:9],
        refs[9:15],
        refs[15:19],
        refs[19],
        refs[20],
    )
    step = 256
    x_scr, qw_scr, kw_scr, vw_scr, cos_scr, sin_scr = scratch
    loads = [
        pltpu.make_async_copy(source, target, load_sems.at[i])
        for i, (source, target) in enumerate(zip(sources[1:], scratch[1:]))
    ]
    chunks = [
        pltpu.make_async_copy(
            sources[0].at[pl.ds(i, step)], x_scr.at[pl.ds(i, step)], load_sems.at[5 + i // step]
        )
        for i in range(0, BLOCK, step)
    ]
    for copy in loads + chunks:
        copy.start()
    for copy in loads:
        copy.wait()
    lane = lax.broadcasted_iota(jnp.int32, (step, 128), 1)
    first_half = (lane & 63) < 32
    left = lane < HEAD_DIM
    here_low = jnp.broadcast_to(yh_ref[0], lane.shape) == 0
    dot = functools.partial(jnp.dot, preferred_element_type=F32)
    mine, kv_send, q_send, q_here = outputs
    sent = []
    for i in range(0, BLOCK, step):
        chunks[i // step].wait()
        at = slice(i, i + step)
        x, cosine, sine = x_scr[at, :], cos_scr[at, :], sin_scr[at, :]

        def turn(values):
            partner = jnp.where(
                first_half, -pltpu.roll(values, 96, 1), pltpu.roll(values, 32, 1)
            )
            return values * cosine + partner * sine

        query = turn(dot(x, qw_scr[...])) * (LOG2E * HEAD_DIM**-0.5)
        key = turn(dot(x, kw_scr[...]))
        value = dot(x, vw_scr[...])
        low = jnp.where(left, key, pltpu.roll(value, 64, 1))
        high = jnp.where(left, pltpu.roll(key, 64, 1), value)
        mine[at, :] = jnp.where(here_low, low, high).astype(BF16)
        kv_send[at, :] = jnp.where(here_low, high, low).astype(BF16)
        low = jnp.where(left, query, 0.0)
        high = jnp.where(left, pltpu.roll(query, 64, 1), 0.0)
        q_here[at, :] = jnp.where(here_low, low, high).astype(BF16)
        sent.append(jnp.where(here_low, high, low))
        if i >= BLOCK // 2:
            both = jnp.where(left, sent[i // step - 2], pltpu.roll(sent[i // step], 64, 1))
            q_send[i - BLOCK // 2 : i - BLOCK // 2 + step, :] = both.astype(BF16)
    targets = (
        results[0].at[pl.ds(0, BLOCK)],
        results[1].at[pl.ds(0, BLOCK)],
        results[1].at[pl.ds(BLOCK, BLOCK // 2)],
        results[2],
    )
    stores = [
        pltpu.make_async_copy(output, target, store_sems.at[i])
        for i, (output, target) in enumerate(zip(outputs, targets))
    ]
    for copy in stores:
        copy.start()
    for copy in stores:
        copy.wait()


def project(yh, rows, q_weight, k_weight, v_weight, cosine, sine):
    block = pltpu.VMEM((BLOCK, 128), BF16)
    table = pltpu.VMEM((BLOCK, 128), F32)
    return pl.pallas_call(
        project_kernel,
        out_shape=(
            pltpu.HBM((PAIR, 128), BF16),
            jax.ShapeDtypeStruct((BLOCK + BLOCK // 2, 128), BF16),
            pltpu.HBM((BLOCK, 128), BF16),
        ),
        in_specs=[pl.BlockSpec(memory_space=pltpu.SMEM)] + [HBM] * 6,
        out_specs=(HBM,) * 3,
        scratch_shapes=[pltpu.VMEM((BLOCK, 1024), BF16)]
        + [block] * 3
        + [table] * 2
        + [block, block, pltpu.VMEM((BLOCK // 2, 128), BF16), block]
        + [pltpu.SemaphoreType.DMA((9,)), pltpu.SemaphoreType.DMA((4,))],
        compiler_params=pltpu.CompilerParams(vmem_limit_bytes=30 << 20),
        name="project",
    )(
        yh,
        *(
            pltpu.with_memory_space_constraint(array, pltpu.HBM)
            for array in (rows, q_weight, k_weight, v_weight, cosine, sine)
        ),
    )


def hot_rows(variate, segment, shape):
    row = lax.broadcasted_iota(jnp.int32, shape, 0)
    variate = jnp.broadcast_to(variate, shape)
    segment = jnp.broadcast_to(segment, shape)
    return row, jnp.where(row < 24, (row & 7) - variate, row - 24 - segment) == 0


def query_side_kernel(at_ref, bias_ref, variate_ref, segment_ref, out_ref):
    for part in range(PAIR // 128):
        block, offset = divmod(part, 8)
        line = at_ref[block] + offset
        row, hot = hot_rows(
            variate_ref[pl.ds(line, 1), :], segment_ref[pl.ds(line, 1), :], (HEAD_DIM, 128)
        )
        bias = jnp.where(row < 8, bias_ref[0], jnp.where(row < 16, bias_ref[1], bias_ref[2]))
        masked = jnp.where(row < 28, MASKED, 0.0)
        columns = jnp.where(row < 24, jnp.where(hot, bias, 0.0), jnp.where(hot, 0.0, masked))
        both = jnp.concatenate([jnp.zeros((HEAD_DIM, 128), F32), columns], axis=0)
        out_ref[part * 128 : (part + 1) * 128, :] = both.T.astype(BF16)
    lane = lax.broadcasted_iota(jnp.int32, (PADDED - PAIR, 128), 1)
    out_ref[PAIR:, :] = jnp.where((lane >= 88) & (lane < 92), MASKED, 0.0).astype(BF16)


def query_side(at, bias, variates, segments):
    smem = pl.BlockSpec(memory_space=pltpu.SMEM)
    vmem = pl.BlockSpec(memory_space=pltpu.VMEM)
    return pl.pallas_call(
        query_side_kernel,
        out_shape=jax.ShapeDtypeStruct((PADDED, 128), BF16),
        in_specs=[smem, smem, vmem, vmem],
        out_specs=vmem,
        name="query_side",
    )(at, bias, variates, segments)


def attend_kernel(
    place_ref, which_ref, start_ref, count_ref, bias_ref, raised_in, *refs, groups, first, last
):
    extra_ref, variate_ref, segment_ref, here_ref, there_ref = refs[:5]
    refs = refs[5:]
    if not first:
        (sums_in, top_in), refs = refs[:2], refs[2:]
    kv_refs, refs = refs[: 2 * groups], refs[2 * groups :]
    if last:
        attended_ref, refs = refs[0], refs[1:]
    else:
        (sums_out, top_out, raised_out), refs = refs[:3], refs[3:]
    (
        sums_scr,
        top_scr,
        near_scr,
        away_scr,
        query_scr,
        kv_scr,
        key_scr,
        value_scr,
        raised_scr,
        state_sem,
        kv_sem,
    ) = refs
    loads = [pltpu.make_async_copy(ref, kv_scr.at[i], kv_sem.at[i]) for i, ref in enumerate(kv_refs)]
    query_loads = [
        pltpu.make_async_copy(here_ref, near_scr, kv_sem.at[2 * groups]),
        pltpu.make_async_copy(
            there_ref.at[pl.ds(BLOCK, BLOCK // 2)], away_scr, kv_sem.at[2 * groups + 1]
        ),
    ]
    for load in query_loads + loads:
        load.start()
    if first:
        sums_scr[...] = jnp.zeros_like(sums_scr)
    else:
        state_load = pltpu.make_async_copy(sums_in, sums_scr, state_sem)
        state_load.start()
    yh, core = place_ref[0], place_ref[1]
    largest = 0.0
    for load in query_loads:
        load.wait()
    left = lax.broadcasted_iota(jnp.int32, (BLOCK // 2, 128), 1) < HEAD_DIM
    near, away = near_scr[...].astype(F32), away_scr[...].astype(F32)
    for row, value in (
        (yh * 2, near[: BLOCK // 2]),
        (yh * 2 + 1, near[BLOCK // 2 :]),
        ((1 - yh) * 2, jnp.where(left, away, 0.0)),
        ((1 - yh) * 2 + 1, jnp.where(left, pltpu.roll(away, 64, 1), 0.0)),
    ):
        at = pl.ds(pl.multiple_of(row * (BLOCK // 2), BLOCK // 2), BLOCK // 2)
        query_scr[at, :] = value.astype(BF16) + extra_ref[at, :]
        largest = jnp.maximum(largest, jnp.max(jnp.sum(value * value, axis=1)))
    query_scr[PAIR:, :] = extra_ref[PAIR:, :]
    raised_scr[0] = raised_in[0]
    allowed = LARGEST - jnp.abs(bias_ref[0])

    for load in loads:
        load.wait()
    def prepare(number, carry):
        name = which_ref[number]

        @pl.when(count_ref[name] > 0)
        def _():
            rows = pl.ds(pl.multiple_of(number % 2 * BLOCK, BLOCK), BLOCK)
            longest = jnp.zeros((1, BLOCK), F32)
            for half in range(2):
                kv = kv_scr[number // 2 * 2 + half, rows, :]
                at = slice(half * BLOCK, (half + 1) * BLOCK)
                lane = lax.broadcasted_iota(jnp.int32, kv.shape, 1)
                value_scr[number, at, :] = jnp.where(lane >= HEAD_DIM, kv, jnp.ones_like(kv))
                keys = kv.T[:HEAD_DIM, :]
                key_scr[number, :HEAD_DIM, at] = keys
                keys = keys.astype(F32)
                longest = jnp.maximum(longest, jnp.sum(keys * keys, axis=0, keepdims=True))
                block = name * 2 + (core if half == 0 else 1 - core)
                for part in range(8):
                    line = pl.ds(block * 8 + part, 1)
                    _, hot = hot_rows(variate_ref[line, :], segment_ref[line, :], (HEAD_DIM, 128))
                    column = half * BLOCK + part * 128
                    key_scr[number, HEAD_DIM:, column : column + 128] = jnp.where(
                        hot, 1.0, 0.0
                    ).astype(BF16)
            within = (allowed > 0) & (1.01 * largest * jnp.max(longest) <= allowed * allowed)
            raised_scr[0] = jnp.where(within, raised_scr[0], 1)

        return carry

    lax.fori_loop(0, 2 * groups, prepare, 0)
    if not first:
        state_load.wait()
    raised = raised_scr[0]
    if not last:
        raised_out[0] = raised

    @pl.when(raised == 0)
    def _():
        def tile(number, carry):
            start = start_ref[which_ref[number]]

            def visit(index, inner):
                at = pl.ds(pl.multiple_of(start + index * ROWS, 64), ROWS)
                scores = jnp.dot(query_scr[at, :], key_scr[number], preferred_element_type=F32)
                weights = jnp.exp2(scores).astype(BF16)
                sums_scr[at, :] += jnp.dot(weights, value_scr[number], preferred_element_type=F32)
                return inner

            return lax.fori_loop(0, count_ref[which_ref[number]], visit, carry)

        lax.fori_loop(0, 2 * groups, tile, 0)

    @pl.when(raised != 0)
    def _():
        top_scr[...] = jnp.zeros_like(top_scr)
        if not first:

            @pl.when(raised_in[0] != 0)
            def _():
                pltpu.sync_copy(top_in, top_scr)

        def tile(number, carry):
            start = start_ref[which_ref[number]]

            def visit(index, inner):
                at = pl.ds(pl.multiple_of(start + index * 256, 64), 256)
                query = query_scr[at, :]

                def part(piece, deep):
                    columns = pl.ds(pl.multiple_of(piece * 256, 256), 256)
                    scores = jnp.dot(
                        query, key_scr[number, :, columns], preferred_element_type=F32
                    )
                    sums = sums_scr[at, :]
                    old = jnp.where(sums[:, :1] > 0, top_scr[at, :], UNSEEN)
                    new = jnp.maximum(old, jnp.max(scores, axis=1, keepdims=True))
                    weights = jnp.exp2(scores - new[:, :1]).astype(BF16)
                    sums_scr[at, :] = sums * jnp.exp2(old - new) + jnp.dot(
                        weights, value_scr[number, columns, :], preferred_element_type=F32
                    )
                    top_scr[at, :] = new
                    return deep

                return lax.fori_loop(0, KEYS // 256, part, inner)

            return lax.fori_loop(0, count_ref[which_ref[number]] * (ROWS // 256), visit, carry)

        lax.fori_loop(0, 2 * groups, tile, 0)
        if not last:
            pltpu.sync_copy(top_scr, top_out)

    if not last:
        pltpu.sync_copy(sums_scr, sums_out)
        return
    left = lax.broadcasted_iota(jnp.int32, (64, 128), 1) < HEAD_DIM
    for part in range(PAIR // 128):
        one = sums_scr[part * 128 : part * 128 + 64, :]
        two = sums_scr[part * 128 + 64 : part * 128 + 128, :]
        value = jnp.where(left, pltpu.roll(one, 64, 1), two)
        total = jnp.where(left, one, pltpu.roll(two, 64, 1))
        attended_ref[part] = (value / total).astype(BF16)


def attend(place, which, start, count, bias, queries, ids, keys_values, state, last):
    groups = len(keys_values) // 2
    first = state is None
    smem = pl.BlockSpec(memory_space=pltpu.SMEM)
    vmem = pl.BlockSpec(memory_space=pltpu.VMEM)
    stay = lambda arrays: tuple(pltpu.with_memory_space_constraint(a, pltpu.HBM) for a in arrays)
    held = queries[:2] + (() if first else state[:2])
    operands = (queries[2],) + ids + stay(held) + tuple(keys_values)
    raised = jnp.zeros((1,), jnp.int32) if first else state[2]
    shape = pltpu.HBM((PADDED, 128), F32)
    if last:
        out_shape, out_specs = jax.ShapeDtypeStruct((16, 64, 128), BF16), vmem
    else:
        out_shape = (shape, shape, jax.ShapeDtypeStruct((1,), jnp.int32))
        out_specs = (HBM, HBM, smem)
    return pl.pallas_call(
        functools.partial(attend_kernel, groups=groups, first=first, last=last),
        out_shape=out_shape,
        in_specs=[smem] * 6 + [vmem] * 3 + [HBM] * (len(operands) - 3),
        out_specs=out_specs,
        input_output_aliases={} if first or last else {11: 0, 12: 1},
        scratch_shapes=[
            pltpu.VMEM((PADDED, 128), F32),
            pltpu.VMEM((PADDED, 128), F32),
            pltpu.VMEM((BLOCK, 128), BF16),
            pltpu.VMEM((BLOCK // 2, 128), BF16),
            pltpu.VMEM((PADDED, 128), BF16),
            pltpu.VMEM((2 * groups, PAIR, 128), BF16),
            pltpu.VMEM((2 * groups, 128, KEYS), BF16),
            pltpu.VMEM((2 * groups, KEYS, 128), BF16),
            pltpu.SMEM((1,), jnp.int32),
            pltpu.SemaphoreType.DMA,
            pltpu.SemaphoreType.DMA((2 * groups + 2,)),
        ],
        compiler_params=pltpu.CompilerParams(vmem_limit_bytes=44 << 20),
        name="attend",
    )(place, which, start, count, bias, raised, *operands)


def out_kernel(
    yl_ref, parts_ref, tokens_ref, gain_ref, shared, resid_ref, ffn_in_ref, rows_scr, weight_scr, sems
):
    loads = []
    for side in range(2):
        half = yl_ref[0] if side == 0 else 1 - yl_ref[0]
        for i in range(8):
            target = pl.ds(pl.multiple_of(half * 512 + i * 64, 64), 64)
            source = shared.at[i, pl.ds(UNITS + side * 64, 64)]
            loads.append(
                pltpu.make_async_copy(source, weight_scr.at[target], sems.at[side * 8 + i])
            )
    for load in loads:
        load.start()
    left = lax.broadcasted_iota(jnp.int32, (64, 128), 1) < HEAD_DIM
    for t in range(8):
        low, high = parts_ref[t].astype(F32), parts_ref[8 + t].astype(F32)
        at = slice(t * 128, (t + 1) * 128)
        rows_scr[:64, at] = jnp.where(left, low, pltpu.roll(high, 64, 1)).astype(BF16)
        rows_scr[64:, at] = jnp.where(left, pltpu.roll(low, 64, 1), high).astype(BF16)
    for load in loads:
        load.wait()
    resid = tokens_ref[...].astype(F32) + jnp.dot(
        rows_scr[...], weight_scr[...], preferred_element_type=F32
    )
    resid_ref[...] = resid
    ffn_in_ref[...] = norm_rows(resid, gain_ref[...]).astype(BF16)


def out_projection(yl, parts, tokens, gain, shared):
    vmem = pl.BlockSpec(memory_space=pltpu.VMEM)
    return pl.pallas_call(
        out_kernel,
        out_shape=(
            jax.ShapeDtypeStruct(tokens.shape, F32),
            jax.ShapeDtypeStruct(tokens.shape, BF16),
        ),
        in_specs=[pl.BlockSpec(memory_space=pltpu.SMEM)] + [vmem] * 3 + [HBM],
        out_specs=(vmem, vmem),
        scratch_shapes=[
            pltpu.VMEM(tokens.shape, BF16),
            pltpu.VMEM((1024, 1024), BF16),
            pltpu.SemaphoreType.DMA((16,)),
        ],
        name="out_projection",
    )(
        yl,
        parts,
        tokens,
        gain.reshape(1, -1),
        pltpu.with_memory_space_constraint(shared, pltpu.HBM),
    )


def ffn_kernel(near_ref, away_ref, shared, own_ref, far_ref, shared_scr, sems):
    copies = [
        pltpu.make_async_copy(shared.at[i, pl.ds(0, UNITS)], shared_scr.at[i], sems.at[i])
        for i in range(shared.shape[0])
    ]
    for copy in copies:
        copy.start()
    dot = functools.partial(jnp.dot, preferred_element_type=F32)
    x = jnp.concatenate([near_ref[...], away_ref[...]], axis=0)
    total = None
    for low in range(0, len(copies), 2):
        copies[low].wait()
        copies[low + 1].wait()
        both = dot(x[:, :512], shared_scr[low, :512, :])
        both = both + dot(x[:, 512:], shared_scr[low + 1, :512, :])
        hidden = (jax.nn.silu(both[:, :512]) * both[:, 512:]).astype(BF16)
        part = dot(hidden[:, :256], shared_scr[low, 512:UNITS, :])
        part = part + dot(hidden[:, 256:], shared_scr[low + 1, 512:UNITS, :])
        total = part if total is None else total + part
    half = total.shape[0] // 2
    own_ref[...] = total[:half]
    far_ref[...] = total[half:].astype(BF16)


def feed_forward(near, away, shared):
    rows, width = near.shape
    vmem = pl.BlockSpec(memory_space=pltpu.VMEM)
    return pl.pallas_call(
        ffn_kernel,
        out_shape=(
            jax.ShapeDtypeStruct((rows, width), F32),
            jax.ShapeDtypeStruct((rows, width), BF16),
        ),
        in_specs=[vmem, vmem, HBM],
        out_specs=(vmem, vmem),
        scratch_shapes=[
            pltpu.VMEM((8, UNITS, 1024), BF16),
            pltpu.SemaphoreType.DMA((8,)),
        ],
        compiler_params=pltpu.CompilerParams(vmem_limit_bytes=40 << 20),
        name="feed_forward",
    )(near, away, pltpu.with_memory_space_constraint(shared, pltpu.HBM))


def per_device(
    tokens,
    segment_ids,
    variate_ids,
    time_ids,
    attn_gain,
    q_weight,
    k_weight,
    v_weight,
    out_weight,
    var_bias,
    ffn_gain,
    gate_weight,
    up_weight,
    down_weight,
):
    z, yh, c = lax.axis_index("z"), lax.axis_index("yh"), lax.axis_index("c")
    pick = functools.partial(lax.dynamic_index_in_dim, keepdims=False)

    swap = [(0, 1), (1, 0)]
    number = lambda *values: jnp.stack(values).astype(jnp.int32)
    lane = lax.broadcasted_iota(jnp.int32, (1, 128), 1)

    with jax.named_scope("gather_normed"):
        normed = norm_rows(tokens, attn_gain).astype(BF16)
        rows = gather_rows(normed, TP, 8)

    with jax.named_scope("tables"):
        freq = 10000.0 ** (-2.0 * (lane & 31).astype(F32) / HEAD_DIM)
        angle = time_ids.astype(F32)[:, None] * freq
        cosine, sine = jnp.cos(angle), jnp.sin(angle)
        bias = pick(var_bias, yh, 1)
        rest = rest_bias = (bias[0] - bias[1]) * LOG2E
        pieces = []
        for _ in range(3):
            piece = lax.reduce_precision(rest, 8, 7)
            pieces.append(piece)
            rest = rest - piece
        take = lax.dynamic_slice_in_dim
        segments = segment_ids.reshape(256, 128)
        variates = variate_ids.reshape(256, 128)
        at = number(z * 32 + c * 8, z * 32 + 16 + c * 8)
        extra = query_side(at, jnp.stack(pieces), variates, segments)
        blocks = segment_ids.reshape(8, 2, 2, BLOCK)
        q_seg = pick(pick(blocks, z, 0), c, 1).reshape(1, PAIR)
        low_seg = segments[::16, :1]
        high_seg = segments[15::16, 127:]
        begin = jnp.sum((q_seg < low_seg).astype(jnp.int32), axis=1)
        end = jnp.sum((q_seg <= high_seg).astype(jnp.int32), axis=1)
        start = begin // 64 * 64
        count = jnp.where(end > begin, (end - start + ROWS - 1) // ROWS, 0)
        out_own = take(out_weight, c * 64, 64)
        out_near = lax.ppermute(out_own, "yl", swap)
        pack = jnp.concatenate(
            [
                jnp.concatenate(
                    [take(gate_weight, c * 512, 512), take(up_weight, c * 512, 512)], axis=1
                ),
                take(down_weight, c * 256, 256),
                out_own,
                out_near,
            ],
            axis=0,
        )
        rows, cosine, sine, extra, start, count, pack = lax.optimization_barrier(
            (rows, cosine, sine, extra, start, count, pack)
        )

    with jax.named_scope("share_weights"):
        shared = lax.all_gather(pack, ("x", "c"), axis=0, tiled=True).reshape(8, UNITS + 128, 1024)

    with jax.named_scope("project"):
        mine, send, q_here = project(
            number(yh), rows, q_weight, k_weight, v_weight, cosine, sine
        )

    with jax.named_scope("exchange"):
        there = lax.ppermute(send, "yh", swap)
        mine = lax.dynamic_update_slice_in_dim(mine, there[:BLOCK], BLOCK, axis=0)

    with jax.named_scope("attention"):
        ahead = lambda array, k: lax.ppermute(array, "z", [(i, (i - k) % 8) for i in range(8)])
        place = number(yh, c)
        gap = rest_bias.reshape(1)
        state = None
        parts = [mine]
        hops = ((0,), (1, 7), (2, 6), (3, 5), (4,))
        for hop, steps in enumerate(hops):
            others = [lax.ppermute(part, "c", swap) for part in parts]
            which = number(
                *((z + k) % 8 * 2 + side for k in steps for side in (yh, 1 - yh))
            )
            coming = [ahead(parts[0], 1)] if hop < 4 else []
            if hop < 3:
                coming.append(ahead(parts[-1], -1))
            state = attend(
                place,
                which,
                start,
                count,
                gap,
                (q_here, there, extra),
                (variates, segments),
                [part for pair in zip(parts, others) for part in pair],
                state,
                hop == 4,
            )
            if hop < 4:
                state, parts = lax.optimization_barrier((state, coming))
        state, shared = lax.optimization_barrier((state, shared))

    with jax.named_scope("to_rows"):
        attended = lax.all_to_all(state, ("yh", "yl", "x"), 0, 0, tiled=True)

    with jax.named_scope("out_projection"):
        resid, ffn_in = out_projection(
            number(lax.axis_index("yl")), attended, tokens, ffn_gain, shared
        )

    with jax.named_scope("feed_forward"):
        own, far = feed_forward(ffn_in, lax.ppermute(ffn_in, "yl", swap), shared)
        back = lax.ppermute(far, "yl", swap)
        return (resid + (own + back.astype(F32))).astype(BF16)


def solution(mesh):
    split = Mesh(mesh.devices.reshape(8, 2, 2, 2, 4), ("z", "yh", "c", "yl", "x"))
    return jax.shard_map(
        per_device,
        mesh=split,
        in_specs=(
            P(REQ + TP, None),
            P(),
            P(),
            P(REQ),
            P(),
            P(None, TP),
            P(None, TP),
            P(None, TP),
            P(TP, None),
            P(None, TP),
            P(),
            P(None, TP),
            P(None, TP),
            P(TP, None),
        ),
        out_specs=P(REQ + TP, None),
        check_vma=False,
    )
```

```python
import functools

import jax
import jax.numpy as jnp
from jax import lax
from jax.experimental import pallas as pl
from jax.experimental.pallas import tpu as pltpu
from jax.sharding import Mesh, PartitionSpec as P

HEAD_DIM = 64
LOG2E = 1.4426950408889634
MASKED = -1e30
UNSEEN = -3e38
LARGEST = 80.0
BLOCK = 1024
KEYS = 2048
ROWS = 512
REQ = ("z", "yh", "c")
TP = ("yl", "x")
UNITS = 768
PAIR = 2 * BLOCK
PADDED = PAIR + ROWS
BF16 = jnp.bfloat16
HBM = pl.BlockSpec(memory_space=pltpu.HBM)
F32 = jnp.float32


def norm_rows(rows, gain):
    values = rows.astype(F32)
    scale = lax.rsqrt(jnp.mean(values * values, axis=-1, keepdims=True) + 1e-05)
    return values * scale * gain


def gather_rows(rows, axes, count):
    copies = jnp.broadcast_to(rows[None], (count,) + rows.shape)
    return lax.all_to_all(
        copies.reshape((count * rows.shape[0],) + rows.shape[1:]), axes, 0, 0, tiled=True
    )


def project_kernel(yh_ref, *refs):
    sources, results, scratch, outputs, load_sems, store_sems = (
        refs[:6],
        refs[6:9],
        refs[9:15],
        refs[15:19],
        refs[19],
        refs[20],
    )
    step = 256
    x_scr, qw_scr, kw_scr, vw_scr, cos_scr, sin_scr = scratch
    loads = [
        pltpu.make_async_copy(source, target, load_sems.at[i])
        for i, (source, target) in enumerate(zip(sources[1:], scratch[1:]))
    ]
    chunks = [
        pltpu.make_async_copy(
            sources[0].at[pl.ds(i, step)], x_scr.at[pl.ds(i, step)], load_sems.at[5 + i // step]
        )
        for i in range(0, BLOCK, step)
    ]
    for copy in loads + chunks:
        copy.start()
    for copy in loads:
        copy.wait()
    lane = lax.broadcasted_iota(jnp.int32, (step, 128), 1)
    first_half = (lane & 63) < 32
    left = lane < HEAD_DIM
    here_low = jnp.broadcast_to(yh_ref[0], lane.shape) == 0
    dot = functools.partial(jnp.dot, preferred_element_type=F32)
    mine, kv_send, q_send, q_here = outputs
    sent = []
    for i in range(0, BLOCK, step):
        chunks[i // step].wait()
        at = slice(i, i + step)
        x, cosine, sine = x_scr[at, :], cos_scr[at, :], sin_scr[at, :]

        def turn(values):
            partner = jnp.where(
                first_half, -pltpu.roll(values, 96, 1), pltpu.roll(values, 32, 1)
            )
            return values * cosine + partner * sine

        query = turn(dot(x, qw_scr[...])) * (LOG2E * HEAD_DIM**-0.5)
        key = turn(dot(x, kw_scr[...]))
        value = dot(x, vw_scr[...])
        low = jnp.where(left, key, pltpu.roll(value, 64, 1))
        high = jnp.where(left, pltpu.roll(key, 64, 1), value)
        mine[at, :] = jnp.where(here_low, low, high).astype(BF16)
        kv_send[at, :] = jnp.where(here_low, high, low).astype(BF16)
        low = jnp.where(left, query, 0.0)
        high = jnp.where(left, pltpu.roll(query, 64, 1), 0.0)
        q_here[at, :] = jnp.where(here_low, low, high).astype(BF16)
        sent.append(jnp.where(here_low, high, low))
        if i >= BLOCK // 2:
            both = jnp.where(left, sent[i // step - 2], pltpu.roll(sent[i // step], 64, 1))
            q_send[i - BLOCK // 2 : i - BLOCK // 2 + step, :] = both.astype(BF16)
    targets = (
        results[0].at[pl.ds(0, BLOCK)],
        results[1].at[pl.ds(0, BLOCK)],
        results[1].at[pl.ds(BLOCK, BLOCK // 2)],
        results[2],
    )
    stores = [
        pltpu.make_async_copy(output, target, store_sems.at[i])
        for i, (output, target) in enumerate(zip(outputs, targets))
    ]
    for copy in stores:
        copy.start()
    for copy in stores:
        copy.wait()


def project(yh, rows, q_weight, k_weight, v_weight, cosine, sine):
    block = pltpu.VMEM((BLOCK, 128), BF16)
    table = pltpu.VMEM((BLOCK, 128), F32)
    return pl.pallas_call(
        project_kernel,
        out_shape=(
            pltpu.HBM((PAIR, 128), BF16),
            jax.ShapeDtypeStruct((BLOCK + BLOCK // 2, 128), BF16),
            pltpu.HBM((BLOCK, 128), BF16),
        ),
        in_specs=[pl.BlockSpec(memory_space=pltpu.SMEM)] + [HBM] * 6,
        out_specs=(HBM,) * 3,
        scratch_shapes=[pltpu.VMEM((BLOCK, 1024), BF16)]
        + [block] * 3
        + [table] * 2
        + [block, block, pltpu.VMEM((BLOCK // 2, 128), BF16), block]
        + [pltpu.SemaphoreType.DMA((9,)), pltpu.SemaphoreType.DMA((4,))],
        compiler_params=pltpu.CompilerParams(vmem_limit_bytes=30 << 20),
        name="project",
    )(
        yh,
        *(
            pltpu.with_memory_space_constraint(array, pltpu.HBM)
            for array in (rows, q_weight, k_weight, v_weight, cosine, sine)
        ),
    )


def hot_rows(variate, segment, shape):
    row = lax.broadcasted_iota(jnp.int32, shape, 0)
    variate = jnp.broadcast_to(variate, shape)
    segment = jnp.broadcast_to(segment, shape)
    return row, jnp.where(row < 24, (row & 7) - variate, row - 24 - segment) == 0


def query_side_kernel(at_ref, bias_ref, variate_ref, segment_ref, out_ref):
    for part in range(PAIR // 128):
        block, offset = divmod(part, 8)
        line = at_ref[block] + offset
        row, hot = hot_rows(
            variate_ref[pl.ds(line, 1), :], segment_ref[pl.ds(line, 1), :], (HEAD_DIM, 128)
        )
        bias = jnp.where(row < 8, bias_ref[0], jnp.where(row < 16, bias_ref[1], bias_ref[2]))
        masked = jnp.where(row < 28, MASKED, 0.0)
        columns = jnp.where(row < 24, jnp.where(hot, bias, 0.0), jnp.where(hot, 0.0, masked))
        both = jnp.concatenate([jnp.zeros((HEAD_DIM, 128), F32), columns], axis=0)
        out_ref[part * 128 : (part + 1) * 128, :] = both.T.astype(BF16)
    lane = lax.broadcasted_iota(jnp.int32, (PADDED - PAIR, 128), 1)
    out_ref[PAIR:, :] = jnp.where((lane >= 88) & (lane < 92), MASKED, 0.0).astype(BF16)


def query_side(at, bias, variates, segments):
    smem = pl.BlockSpec(memory_space=pltpu.SMEM)
    vmem = pl.BlockSpec(memory_space=pltpu.VMEM)
    return pl.pallas_call(
        query_side_kernel,
        out_shape=jax.ShapeDtypeStruct((PADDED, 128), BF16),
        in_specs=[smem, smem, vmem, vmem],
        out_specs=vmem,
        name="query_side",
    )(at, bias, variates, segments)


def attend_kernel(
    place_ref, which_ref, start_ref, count_ref, bias_ref, raised_in, *refs, groups, first, last
):
    extra_ref, variate_ref, segment_ref, here_ref, there_ref = refs[:5]
    refs = refs[5:]
    if not first:
        (sums_in, top_in), refs = refs[:2], refs[2:]
    kv_refs, refs = refs[: 2 * groups], refs[2 * groups :]
    if last:
        attended_ref, refs = refs[0], refs[1:]
    else:
        (sums_out, top_out, raised_out), refs = refs[:3], refs[3:]
    (
        sums_scr,
        top_scr,
        near_scr,
        away_scr,
        query_scr,
        kv_scr,
        key_scr,
        value_scr,
        raised_scr,
        state_sem,
        kv_sem,
    ) = refs
    loads = [pltpu.make_async_copy(ref, kv_scr.at[i], kv_sem.at[i]) for i, ref in enumerate(kv_refs)]
    query_loads = [
        pltpu.make_async_copy(here_ref, near_scr, kv_sem.at[2 * groups]),
        pltpu.make_async_copy(
            there_ref.at[pl.ds(BLOCK, BLOCK // 2)], away_scr, kv_sem.at[2 * groups + 1]
        ),
    ]
    for load in query_loads + loads:
        load.start()
    if first:
        sums_scr[...] = jnp.zeros_like(sums_scr)
    else:
        state_load = pltpu.make_async_copy(sums_in, sums_scr, state_sem)
        state_load.start()
    yh, core = place_ref[0], place_ref[1]
    largest = 0.0
    for load in query_loads:
        load.wait()
    left = lax.broadcasted_iota(jnp.int32, (BLOCK // 2, 128), 1) < HEAD_DIM
    near, away = near_scr[...].astype(F32), away_scr[...].astype(F32)
    for row, value in (
        (yh * 2, near[: BLOCK // 2]),
        (yh * 2 + 1, near[BLOCK // 2 :]),
        ((1 - yh) * 2, jnp.where(left, away, 0.0)),
        ((1 - yh) * 2 + 1, jnp.where(left, pltpu.roll(away, 64, 1), 0.0)),
    ):
        at = pl.ds(pl.multiple_of(row * (BLOCK // 2), BLOCK // 2), BLOCK // 2)
        query_scr[at, :] = value.astype(BF16) + extra_ref[at, :]
        largest = jnp.maximum(largest, jnp.max(jnp.sum(value * value, axis=1)))
    query_scr[PAIR:, :] = extra_ref[PAIR:, :]
    raised_scr[0] = raised_in[0]
    allowed = LARGEST - jnp.abs(bias_ref[0])

    for load in loads:
        load.wait()
    def prepare(number, carry):
        name = which_ref[number]

        @pl.when(count_ref[name] > 0)
        def _():
            rows = pl.ds(pl.multiple_of(number % 2 * BLOCK, BLOCK), BLOCK)
            longest = jnp.zeros((1, BLOCK), F32)
            for half in range(2):
                kv = kv_scr[number // 2 * 2 + half, rows, :]
                at = slice(half * BLOCK, (half + 1) * BLOCK)
                lane = lax.broadcasted_iota(jnp.int32, kv.shape, 1)
                value_scr[number, at, :] = jnp.where(lane >= HEAD_DIM, kv, jnp.ones_like(kv))
                keys = kv.T[:HEAD_DIM, :]
                key_scr[number, :HEAD_DIM, at] = keys
                keys = keys.astype(F32)
                longest = jnp.maximum(longest, jnp.sum(keys * keys, axis=0, keepdims=True))
                block = name * 2 + (core if half == 0 else 1 - core)
                for part in range(8):
                    line = pl.ds(block * 8 + part, 1)
                    _, hot = hot_rows(variate_ref[line, :], segment_ref[line, :], (HEAD_DIM, 128))
                    column = half * BLOCK + part * 128
                    key_scr[number, HEAD_DIM:, column : column + 128] = jnp.where(
                        hot, 1.0, 0.0
                    ).astype(BF16)
            within = (allowed > 0) & (1.01 * largest * jnp.max(longest) <= allowed * allowed)
            raised_scr[0] = jnp.where(within, raised_scr[0], 1)

        return carry

    lax.fori_loop(0, 2 * groups, prepare, 0)
    if not first:
        state_load.wait()
    raised = raised_scr[0]
    if not last:
        raised_out[0] = raised

    @pl.when(raised == 0)
    def _():
        def tile(number, carry):
            start = start_ref[which_ref[number]]

            def visit(index, inner):
                at = pl.ds(pl.multiple_of(start + index * ROWS, 64), ROWS)
                scores = jnp.dot(query_scr[at, :], key_scr[number], preferred_element_type=F32)
                weights = jnp.exp2(scores).astype(BF16)
                sums_scr[at, :] += jnp.dot(weights, value_scr[number], preferred_element_type=F32)
                return inner

            return lax.fori_loop(0, count_ref[which_ref[number]], visit, carry)

        lax.fori_loop(0, 2 * groups, tile, 0)

    @pl.when(raised != 0)
    def _():
        top_scr[...] = jnp.zeros_like(top_scr)
        if not first:

            @pl.when(raised_in[0] != 0)
            def _():
                pltpu.sync_copy(top_in, top_scr)

        def tile(number, carry):
            start = start_ref[which_ref[number]]

            def visit(index, inner):
                at = pl.ds(pl.multiple_of(start + index * 256, 64), 256)
                query = query_scr[at, :]

                def part(piece, deep):
                    columns = pl.ds(pl.multiple_of(piece * 256, 256), 256)
                    scores = jnp.dot(
                        query, key_scr[number, :, columns], preferred_element_type=F32
                    )
                    sums = sums_scr[at, :]
                    old = jnp.where(sums[:, :1] > 0, top_scr[at, :], UNSEEN)
                    new = jnp.maximum(old, jnp.max(scores, axis=1, keepdims=True))
                    weights = jnp.exp2(scores - new[:, :1]).astype(BF16)
                    sums_scr[at, :] = sums * jnp.exp2(old - new) + jnp.dot(
                        weights, value_scr[number, columns, :], preferred_element_type=F32
                    )
                    top_scr[at, :] = new
                    return deep

                return lax.fori_loop(0, KEYS // 256, part, inner)

            return lax.fori_loop(0, count_ref[which_ref[number]] * (ROWS // 256), visit, carry)

        lax.fori_loop(0, 2 * groups, tile, 0)
        if not last:
            pltpu.sync_copy(top_scr, top_out)

    if not last:
        pltpu.sync_copy(sums_scr, sums_out)
        return
    left = lax.broadcasted_iota(jnp.int32, (64, 128), 1) < HEAD_DIM
    for part in range(PAIR // 128):
        one = sums_scr[part * 128 : part * 128 + 64, :]
        two = sums_scr[part * 128 + 64 : part * 128 + 128, :]
        value = jnp.where(left, pltpu.roll(one, 64, 1), two)
        total = jnp.where(left, one, pltpu.roll(two, 64, 1))
        attended_ref[part] = (value / total).astype(BF16)


def attend(place, which, start, count, bias, queries, ids, keys_values, state, last):
    groups = len(keys_values) // 2
    first = state is None
    smem = pl.BlockSpec(memory_space=pltpu.SMEM)
    vmem = pl.BlockSpec(memory_space=pltpu.VMEM)
    stay = lambda arrays: tuple(pltpu.with_memory_space_constraint(a, pltpu.HBM) for a in arrays)
    held = queries[:2] + (() if first else state[:2])
    kept = 1 if first else 0
    operands = (queries[2],) + ids + stay(held)
    operands = operands + stay(keys_values[:kept]) + tuple(keys_values[kept:])
    raised = jnp.zeros((1,), jnp.int32) if first else state[2]
    shape = pltpu.HBM((PADDED, 128), F32)
    if last:
        out_shape, out_specs = jax.ShapeDtypeStruct((16, 64, 128), BF16), vmem
    else:
        out_shape = (shape, shape, jax.ShapeDtypeStruct((1,), jnp.int32))
        out_specs = (HBM, HBM, smem)
    return pl.pallas_call(
        functools.partial(attend_kernel, groups=groups, first=first, last=last),
        out_shape=out_shape,
        in_specs=[smem] * 6 + [vmem] * 3 + [HBM] * (len(operands) - 3),
        out_specs=out_specs,
        input_output_aliases={} if first or last else {11: 0, 12: 1},
        scratch_shapes=[
            pltpu.VMEM((PADDED, 128), F32),
            pltpu.VMEM((PADDED, 128), F32),
            pltpu.VMEM((BLOCK, 128), BF16),
            pltpu.VMEM((BLOCK // 2, 128), BF16),
            pltpu.VMEM((PADDED, 128), BF16),
            pltpu.VMEM((2 * groups, PAIR, 128), BF16),
            pltpu.VMEM((2 * groups, 128, KEYS), BF16),
            pltpu.VMEM((2 * groups, KEYS, 128), BF16),
            pltpu.SMEM((1,), jnp.int32),
            pltpu.SemaphoreType.DMA,
            pltpu.SemaphoreType.DMA((2 * groups + 2,)),
        ],
        compiler_params=pltpu.CompilerParams(vmem_limit_bytes=44 << 20),
        name="attend",
    )(place, which, start, count, bias, raised, *operands)


def out_kernel(
    yl_ref, parts_ref, tokens_ref, gain_ref, shared, resid_ref, ffn_in_ref, rows_scr, weight_scr, sems
):
    loads = []
    for side in range(2):
        half = yl_ref[0] if side == 0 else 1 - yl_ref[0]
        for i in range(8):
            target = pl.ds(pl.multiple_of(half * 512 + i * 64, 64), 64)
            source = shared.at[i, pl.ds(UNITS + side * 64, 64)]
            loads.append(
                pltpu.make_async_copy(source, weight_scr.at[target], sems.at[side * 8 + i])
            )
    for load in loads:
        load.start()
    left = lax.broadcasted_iota(jnp.int32, (64, 128), 1) < HEAD_DIM
    for t in range(8):
        low, high = parts_ref[t].astype(F32), parts_ref[8 + t].astype(F32)
        at = slice(t * 128, (t + 1) * 128)
        rows_scr[:64, at] = jnp.where(left, low, pltpu.roll(high, 64, 1)).astype(BF16)
        rows_scr[64:, at] = jnp.where(left, pltpu.roll(low, 64, 1), high).astype(BF16)
    for load in loads:
        load.wait()
    resid = tokens_ref[...].astype(F32) + jnp.dot(
        rows_scr[...], weight_scr[...], preferred_element_type=F32
    )
    resid_ref[...] = resid
    ffn_in_ref[...] = norm_rows(resid, gain_ref[...]).astype(BF16)


def out_projection(yl, parts, tokens, gain, shared):
    vmem = pl.BlockSpec(memory_space=pltpu.VMEM)
    return pl.pallas_call(
        out_kernel,
        out_shape=(
            jax.ShapeDtypeStruct(tokens.shape, F32),
            jax.ShapeDtypeStruct(tokens.shape, BF16),
        ),
        in_specs=[pl.BlockSpec(memory_space=pltpu.SMEM)] + [vmem] * 3 + [HBM],
        out_specs=(vmem, vmem),
        scratch_shapes=[
            pltpu.VMEM(tokens.shape, BF16),
            pltpu.VMEM((1024, 1024), BF16),
            pltpu.SemaphoreType.DMA((16,)),
        ],
        name="out_projection",
    )(
        yl,
        parts,
        tokens,
        gain.reshape(1, -1),
        pltpu.with_memory_space_constraint(shared, pltpu.HBM),
    )


def ffn_kernel(near_ref, away_ref, shared, own_ref, far_ref, near_scr, shared_scr, sems):
    near_load = pltpu.make_async_copy(near_ref, near_scr, sems.at[8])
    near_load.start()
    copies = [
        pltpu.make_async_copy(shared.at[i, pl.ds(0, UNITS)], shared_scr.at[i], sems.at[i])
        for i in range(shared.shape[0])
    ]
    for copy in copies:
        copy.start()
    dot = functools.partial(jnp.dot, preferred_element_type=F32)
    near_load.wait()
    x = jnp.concatenate([near_scr[...], away_ref[...]], axis=0)
    total = None
    for low in range(0, len(copies), 2):
        copies[low].wait()
        copies[low + 1].wait()
        both = dot(x[:, :512], shared_scr[low, :512, :])
        both = both + dot(x[:, 512:], shared_scr[low + 1, :512, :])
        hidden = (jax.nn.silu(both[:, :512]) * both[:, 512:]).astype(BF16)
        part = dot(hidden[:, :256], shared_scr[low, 512:UNITS, :])
        part = part + dot(hidden[:, 256:], shared_scr[low + 1, 512:UNITS, :])
        total = part if total is None else total + part
    half = total.shape[0] // 2
    own_ref[...] = total[:half]
    far_ref[...] = total[half:].astype(BF16)


def feed_forward(near, away, shared):
    rows, width = near.shape
    vmem = pl.BlockSpec(memory_space=pltpu.VMEM)
    return pl.pallas_call(
        ffn_kernel,
        out_shape=(
            jax.ShapeDtypeStruct((rows, width), F32),
            jax.ShapeDtypeStruct((rows, width), BF16),
        ),
        in_specs=[HBM, vmem, HBM],
        out_specs=(vmem, vmem),
        scratch_shapes=[
            pltpu.VMEM(near.shape, BF16),
            pltpu.VMEM((8, UNITS, 1024), BF16),
            pltpu.SemaphoreType.DMA((9,)),
        ],
        compiler_params=pltpu.CompilerParams(vmem_limit_bytes=40 << 20),
        name="feed_forward",
    )(
        pltpu.with_memory_space_constraint(near, pltpu.HBM),
        away,
        pltpu.with_memory_space_constraint(shared, pltpu.HBM),
    )


def per_device(
    tokens,
    segment_ids,
    variate_ids,
    time_ids,
    attn_gain,
    q_weight,
    k_weight,
    v_weight,
    out_weight,
    var_bias,
    ffn_gain,
    gate_weight,
    up_weight,
    down_weight,
):
    z, yh, c = lax.axis_index("z"), lax.axis_index("yh"), lax.axis_index("c")
    pick = functools.partial(lax.dynamic_index_in_dim, keepdims=False)

    swap = [(0, 1), (1, 0)]
    number = lambda *values: jnp.stack(values).astype(jnp.int32)
    lane = lax.broadcasted_iota(jnp.int32, (1, 128), 1)

    with jax.named_scope("gather_normed"):
        normed = norm_rows(tokens, attn_gain).astype(BF16)
        rows = gather_rows(normed, TP, 8)

    with jax.named_scope("tables"):
        freq = 10000.0 ** (-2.0 * (lane & 31).astype(F32) / HEAD_DIM)
        angle = time_ids.astype(F32)[:, None] * freq
        cosine, sine = jnp.cos(angle), jnp.sin(angle)
        bias = pick(var_bias, yh, 1)
        rest = rest_bias = (bias[0] - bias[1]) * LOG2E
        pieces = []
        for _ in range(3):
            piece = lax.reduce_precision(rest, 8, 7)
            pieces.append(piece)
            rest = rest - piece
        take = lax.dynamic_slice_in_dim
        segments = segment_ids.reshape(256, 128)
        variates = variate_ids.reshape(256, 128)
        at = number(z * 32 + c * 8, z * 32 + 16 + c * 8)
        extra = query_side(at, jnp.stack(pieces), variates, segments)
        blocks = segment_ids.reshape(8, 2, 2, BLOCK)
        q_seg = pick(pick(blocks, z, 0), c, 1).reshape(1, PAIR)
        low_seg = segments[::16, :1]
        high_seg = segments[15::16, 127:]
        begin = jnp.sum((q_seg < low_seg).astype(jnp.int32), axis=1)
        end = jnp.sum((q_seg <= high_seg).astype(jnp.int32), axis=1)
        start = begin // 64 * 64
        count = jnp.where(end > begin, (end - start + ROWS - 1) // ROWS, 0)
        out_own = take(out_weight, c * 64, 64)
        out_near = lax.ppermute(out_own, "yl", swap)
        pack = jnp.concatenate(
            [
                jnp.concatenate(
                    [take(gate_weight, c * 512, 512), take(up_weight, c * 512, 512)], axis=1
                ),
                take(down_weight, c * 256, 256),
                out_own,
                out_near,
            ],
            axis=0,
        )
        rows, cosine, sine, extra, start, count, pack = lax.optimization_barrier(
            (rows, cosine, sine, extra, start, count, pack)
        )

    with jax.named_scope("share_weights"):
        shared = lax.all_gather(pack, ("x", "c"), axis=0, tiled=True).reshape(8, UNITS + 128, 1024)

    with jax.named_scope("project"):
        mine, send, q_here = project(
            number(yh), rows, q_weight, k_weight, v_weight, cosine, sine
        )

    with jax.named_scope("exchange"):
        there = lax.ppermute(send, "yh", swap)
        mine = lax.dynamic_update_slice_in_dim(mine, there[:BLOCK], BLOCK, axis=0)

    with jax.named_scope("attention"):
        ahead = lambda array, k: lax.ppermute(array, "z", [(i, (i - k) % 8) for i in range(8)])
        place = number(yh, c)
        gap = rest_bias.reshape(1)
        state = None
        parts = [mine]
        hops = ((0,), (1, 7), (2, 6), (3, 5), (4,))
        for hop, steps in enumerate(hops):
            others = [lax.ppermute(part, "c", swap) for part in parts]
            which = number(
                *((z + k) % 8 * 2 + side for k in steps for side in (yh, 1 - yh))
            )
            coming = [ahead(parts[0], 1)] if hop < 4 else []
            if hop < 3:
                coming.append(ahead(parts[-1], -1))
            state = attend(
                place,
                which,
                start,
                count,
                gap,
                (q_here, there, extra),
                (variates, segments),
                [part for pair in zip(parts, others) for part in pair],
                state,
                hop == 4,
            )
            if hop < 4:
                state, parts = lax.optimization_barrier((state, coming))
        state, shared = lax.optimization_barrier((state, shared))

    with jax.named_scope("to_rows"):
        attended = lax.all_to_all(state, ("yh", "yl", "x"), 0, 0, tiled=True)

    with jax.named_scope("out_projection"):
        resid, ffn_in = out_projection(
            number(lax.axis_index("yl")), attended, tokens, ffn_gain, shared
        )

    with jax.named_scope("feed_forward"):
        own, far = feed_forward(ffn_in, lax.ppermute(ffn_in, "yl", swap), shared)
        back = lax.ppermute(far, "yl", swap)
        return (resid + (own + back.astype(F32))).astype(BF16)


def solution(mesh):
    split = Mesh(mesh.devices.reshape(8, 2, 2, 2, 4), ("z", "yh", "c", "yl", "x"))
    return jax.shard_map(
        per_device,
        mesh=split,
        in_specs=(
            P(REQ + TP, None),
            P(),
            P(),
            P(REQ),
            P(),
            P(None, TP),
            P(None, TP),
            P(None, TP),
            P(TP, None),
            P(None, TP),
            P(),
            P(None, TP),
            P(None, TP),
            P(TP, None),
        ),
        out_specs=P(REQ + TP, None),
        check_vma=False,
    )
```

```python
import functools

import jax
import jax.numpy as jnp
from jax import lax
from jax.experimental import pallas as pl
from jax.experimental.pallas import tpu as pltpu
from jax.sharding import Mesh, PartitionSpec as P

HEAD_DIM = 64
LOG2E = 1.4426950408889634
MASKED = -1e30
UNSEEN = -3e38
LARGEST = 80.0
BLOCK = 1024
KEYS = 2048
ROWS = 512
REQ = ("z", "yh", "c")
TP = ("yl", "x")
UNITS = 768
PAIR = 2 * BLOCK
PADDED = PAIR + ROWS
BF16 = jnp.bfloat16
HBM = pl.BlockSpec(memory_space=pltpu.HBM)
F32 = jnp.float32


def norm_rows(rows, gain):
    values = rows.astype(F32)
    scale = lax.rsqrt(jnp.mean(values * values, axis=-1, keepdims=True) + 1e-05)
    return values * scale * gain


def gather_rows(rows, axes, count):
    copies = jnp.broadcast_to(rows[None], (count,) + rows.shape)
    return lax.all_to_all(
        copies.reshape((count * rows.shape[0],) + rows.shape[1:]), axes, 0, 0, tiled=True
    )


def project_kernel(yh_ref, *refs):
    sources, results, scratch, outputs, load_sems, store_sems = (
        refs[:6],
        refs[6:9],
        refs[9:15],
        refs[15:19],
        refs[19],
        refs[20],
    )
    step = 256
    x_scr, qw_scr, kw_scr, vw_scr, cos_scr, sin_scr = scratch
    loads = [
        pltpu.make_async_copy(source, target, load_sems.at[i])
        for i, (source, target) in enumerate(zip(sources[1:], scratch[1:]))
    ]
    chunks = [
        pltpu.make_async_copy(
            sources[0].at[pl.ds(i, step)], x_scr.at[pl.ds(i, step)], load_sems.at[5 + i // step]
        )
        for i in range(0, BLOCK, step)
    ]
    for copy in loads + chunks:
        copy.start()
    for copy in loads:
        copy.wait()
    lane = lax.broadcasted_iota(jnp.int32, (step, 128), 1)
    first_half = (lane & 63) < 32
    left = lane < HEAD_DIM
    here_low = jnp.broadcast_to(yh_ref[0], lane.shape) == 0
    dot = functools.partial(jnp.dot, preferred_element_type=F32)
    mine, kv_send, q_send, q_here = outputs
    sent = []
    for i in range(0, BLOCK, step):
        chunks[i // step].wait()
        at = slice(i, i + step)
        x, cosine, sine = x_scr[at, :], cos_scr[at, :], sin_scr[at, :]

        def turn(values):
            partner = jnp.where(
                first_half, -pltpu.roll(values, 96, 1), pltpu.roll(values, 32, 1)
            )
            return values * cosine + partner * sine

        query = turn(dot(x, qw_scr[...])) * (LOG2E * HEAD_DIM**-0.5)
        key = turn(dot(x, kw_scr[...]))
        value = dot(x, vw_scr[...])
        low = jnp.where(left, key, pltpu.roll(value, 64, 1))
        high = jnp.where(left, pltpu.roll(key, 64, 1), value)
        mine[at, :] = jnp.where(here_low, low, high).astype(BF16)
        kv_send[at, :] = jnp.where(here_low, high, low).astype(BF16)
        low = jnp.where(left, query, 0.0)
        high = jnp.where(left, pltpu.roll(query, 64, 1), 0.0)
        q_here[at, :] = jnp.where(here_low, low, high).astype(BF16)
        sent.append(jnp.where(here_low, high, low))
        if i >= BLOCK // 2:
            both = jnp.where(left, sent[i // step - 2], pltpu.roll(sent[i // step], 64, 1))
            q_send[i - BLOCK // 2 : i - BLOCK // 2 + step, :] = both.astype(BF16)
    targets = (
        results[0].at[pl.ds(0, BLOCK)],
        results[1].at[pl.ds(0, BLOCK)],
        results[1].at[pl.ds(BLOCK, BLOCK // 2)],
        results[2],
    )
    stores = [
        pltpu.make_async_copy(output, target, store_sems.at[i])
        for i, (output, target) in enumerate(zip(outputs, targets))
    ]
    for copy in stores:
        copy.start()
    for copy in stores:
        copy.wait()


def project(yh, rows, q_weight, k_weight, v_weight, cosine, sine):
    block = pltpu.VMEM((BLOCK, 128), BF16)
    table = pltpu.VMEM((BLOCK, 128), F32)
    return pl.pallas_call(
        project_kernel,
        out_shape=(
            pltpu.HBM((PAIR, 128), BF16),
            jax.ShapeDtypeStruct((BLOCK + BLOCK // 2, 128), BF16),
            pltpu.HBM((BLOCK, 128), BF16),
        ),
        in_specs=[pl.BlockSpec(memory_space=pltpu.SMEM)] + [HBM] * 6,
        out_specs=(HBM,) * 3,
        scratch_shapes=[pltpu.VMEM((BLOCK, 1024), BF16)]
        + [block] * 3
        + [table] * 2
        + [block, block, pltpu.VMEM((BLOCK // 2, 128), BF16), block]
        + [pltpu.SemaphoreType.DMA((9,)), pltpu.SemaphoreType.DMA((4,))],
        compiler_params=pltpu.CompilerParams(vmem_limit_bytes=30 << 20),
        name="project",
    )(
        yh,
        *(
            pltpu.with_memory_space_constraint(array, pltpu.HBM)
            for array in (rows, q_weight, k_weight, v_weight, cosine, sine)
        ),
    )


def hot_rows(variate, segment, shape):
    row = lax.broadcasted_iota(jnp.int32, shape, 0)
    variate = jnp.broadcast_to(variate, shape)
    segment = jnp.broadcast_to(segment, shape)
    return row, jnp.where(row < 24, (row & 7) - variate, row - 24 - segment) == 0


def query_side_kernel(at_ref, bias_ref, variate_ref, segment_ref, out_ref):
    for part in range(PAIR // 128):
        block, offset = divmod(part, 8)
        line = at_ref[block] + offset
        row, hot = hot_rows(
            variate_ref[pl.ds(line, 1), :], segment_ref[pl.ds(line, 1), :], (HEAD_DIM, 128)
        )
        bias = jnp.where(row < 8, bias_ref[0], jnp.where(row < 16, bias_ref[1], bias_ref[2]))
        masked = jnp.where(row < 28, MASKED, 0.0)
        columns = jnp.where(row < 24, jnp.where(hot, bias, 0.0), jnp.where(hot, 0.0, masked))
        both = jnp.concatenate([jnp.zeros((HEAD_DIM, 128), F32), columns], axis=0)
        out_ref[part * 128 : (part + 1) * 128, :] = both.T.astype(BF16)
    lane = lax.broadcasted_iota(jnp.int32, (PADDED - PAIR, 128), 1)
    out_ref[PAIR:, :] = jnp.where((lane >= 88) & (lane < 92), MASKED, 0.0).astype(BF16)


def query_side(at, bias, variates, segments):
    smem = pl.BlockSpec(memory_space=pltpu.SMEM)
    vmem = pl.BlockSpec(memory_space=pltpu.VMEM)
    return pl.pallas_call(
        query_side_kernel,
        out_shape=jax.ShapeDtypeStruct((PADDED, 128), BF16),
        in_specs=[smem, smem, vmem, vmem],
        out_specs=vmem,
        name="query_side",
    )(at, bias, variates, segments)


def attend_kernel(
    place_ref, which_ref, start_ref, count_ref, bias_ref, raised_in, *refs, groups, first, last
):
    extra_ref, variate_ref, segment_ref, here_ref, there_ref = refs[:5]
    refs = refs[5:]
    if not first:
        (sums_in, top_in), refs = refs[:2], refs[2:]
    kv_refs, refs = refs[: 2 * groups], refs[2 * groups :]
    if last:
        attended_ref, refs = refs[0], refs[1:]
    else:
        (sums_out, top_out, raised_out), refs = refs[:3], refs[3:]
    (
        sums_scr,
        top_scr,
        near_scr,
        away_scr,
        query_scr,
        kv_scr,
        key_scr,
        value_scr,
        raised_scr,
        state_sem,
        kv_sem,
    ) = refs
    loads = [pltpu.make_async_copy(ref, kv_scr.at[i], kv_sem.at[i]) for i, ref in enumerate(kv_refs)]
    query_loads = [
        pltpu.make_async_copy(here_ref, near_scr, kv_sem.at[2 * groups]),
        pltpu.make_async_copy(
            there_ref.at[pl.ds(BLOCK, BLOCK // 2)], away_scr, kv_sem.at[2 * groups + 1]
        ),
    ]
    for load in query_loads + loads:
        load.start()
    if first:
        sums_scr[...] = jnp.zeros_like(sums_scr)
    else:
        state_load = pltpu.make_async_copy(sums_in, sums_scr, state_sem)
        state_load.start()
    yh, core = place_ref[0], place_ref[1]
    largest = 0.0
    for load in query_loads:
        load.wait()
    left = lax.broadcasted_iota(jnp.int32, (BLOCK // 2, 128), 1) < HEAD_DIM
    near, away = near_scr[...].astype(F32), away_scr[...].astype(F32)
    for row, value in (
        (yh * 2, near[: BLOCK // 2]),
        (yh * 2 + 1, near[BLOCK // 2 :]),
        ((1 - yh) * 2, jnp.where(left, away, 0.0)),
        ((1 - yh) * 2 + 1, jnp.where(left, pltpu.roll(away, 64, 1), 0.0)),
    ):
        at = pl.ds(pl.multiple_of(row * (BLOCK // 2), BLOCK // 2), BLOCK // 2)
        query_scr[at, :] = value.astype(BF16) + extra_ref[at, :]
        largest = jnp.maximum(largest, jnp.max(jnp.sum(value * value, axis=1)))
    query_scr[PAIR:, :] = extra_ref[PAIR:, :]
    raised_scr[0] = raised_in[0]
    allowed = LARGEST - jnp.abs(bias_ref[0])

    for load in loads:
        load.wait()
    def prepare(number, carry):
        name = which_ref[number]

        @pl.when(count_ref[name] > 0)
        def _():
            rows = pl.ds(pl.multiple_of(number % 2 * BLOCK, BLOCK), BLOCK)
            longest = jnp.zeros((1, BLOCK), F32)
            for half in range(2):
                kv = kv_scr[number // 2 * 2 + half, rows, :]
                at = slice(half * BLOCK, (half + 1) * BLOCK)
                lane = lax.broadcasted_iota(jnp.int32, kv.shape, 1)
                value_scr[number, at, :] = jnp.where(lane >= HEAD_DIM, kv, jnp.ones_like(kv))
                keys = kv.T[:HEAD_DIM, :]
                key_scr[number, :HEAD_DIM, at] = keys
                keys = keys.astype(F32)
                longest = jnp.maximum(longest, jnp.sum(keys * keys, axis=0, keepdims=True))
                block = name * 2 + (core if half == 0 else 1 - core)
                for part in range(8):
                    line = pl.ds(block * 8 + part, 1)
                    _, hot = hot_rows(variate_ref[line, :], segment_ref[line, :], (HEAD_DIM, 128))
                    column = half * BLOCK + part * 128
                    key_scr[number, HEAD_DIM:, column : column + 128] = jnp.where(
                        hot, 1.0, 0.0
                    ).astype(BF16)
            within = (allowed > 0) & (1.01 * largest * jnp.max(longest) <= allowed * allowed)
            raised_scr[0] = jnp.where(within, raised_scr[0], 1)

        return carry

    lax.fori_loop(0, 2 * groups, prepare, 0)
    if not first:
        state_load.wait()
    raised = raised_scr[0]
    if not last:
        raised_out[0] = raised

    @pl.when(raised == 0)
    def _():
        def tile(number, carry):
            start = start_ref[which_ref[number]]

            def visit(index, inner):
                at = pl.ds(pl.multiple_of(start + index * ROWS, 64), ROWS)
                scores = jnp.dot(query_scr[at, :], key_scr[number], preferred_element_type=F32)
                weights = jnp.exp2(scores).astype(BF16)
                sums_scr[at, :] += jnp.dot(weights, value_scr[number], preferred_element_type=F32)
                return inner

            return lax.fori_loop(0, count_ref[which_ref[number]], visit, carry)

        lax.fori_loop(0, 2 * groups, tile, 0)

    @pl.when(raised != 0)
    def _():
        top_scr[...] = jnp.zeros_like(top_scr)
        if not first:

            @pl.when(raised_in[0] != 0)
            def _():
                pltpu.sync_copy(top_in, top_scr)

        def tile(number, carry):
            start = start_ref[which_ref[number]]

            def visit(index, inner):
                at = pl.ds(pl.multiple_of(start + index * 256, 64), 256)
                query = query_scr[at, :]

                def part(piece, deep):
                    columns = pl.ds(pl.multiple_of(piece * 256, 256), 256)
                    scores = jnp.dot(
                        query, key_scr[number, :, columns], preferred_element_type=F32
                    )
                    sums = sums_scr[at, :]
                    old = jnp.where(sums[:, :1] > 0, top_scr[at, :], UNSEEN)
                    new = jnp.maximum(old, jnp.max(scores, axis=1, keepdims=True))
                    weights = jnp.exp2(scores - new[:, :1]).astype(BF16)
                    sums_scr[at, :] = sums * jnp.exp2(old - new) + jnp.dot(
                        weights, value_scr[number, columns, :], preferred_element_type=F32
                    )
                    top_scr[at, :] = new
                    return deep

                return lax.fori_loop(0, KEYS // 256, part, inner)

            return lax.fori_loop(0, count_ref[which_ref[number]] * (ROWS // 256), visit, carry)

        lax.fori_loop(0, 2 * groups, tile, 0)
        if not last:
            pltpu.sync_copy(top_scr, top_out)

    if not last:
        pltpu.sync_copy(sums_scr, sums_out)
        return
    left = lax.broadcasted_iota(jnp.int32, (64, 128), 1) < HEAD_DIM
    for part in range(PAIR // 128):
        one = sums_scr[part * 128 : part * 128 + 64, :]
        two = sums_scr[part * 128 + 64 : part * 128 + 128, :]
        value = jnp.where(left, pltpu.roll(one, 64, 1), two)
        total = jnp.where(left, one, pltpu.roll(two, 64, 1))
        attended_ref[part] = (value / total).astype(BF16)


def attend(place, which, start, count, bias, queries, ids, keys_values, state, last):
    groups = len(keys_values) // 2
    first = state is None
    smem = pl.BlockSpec(memory_space=pltpu.SMEM)
    vmem = pl.BlockSpec(memory_space=pltpu.VMEM)
    stay = lambda arrays: tuple(pltpu.with_memory_space_constraint(a, pltpu.HBM) for a in arrays)
    held = queries[:2] + (() if first else state[:2])
    kept = 1 if first else 0
    operands = (queries[2],) + ids + stay(held)
    operands = operands + stay(keys_values[:kept]) + tuple(keys_values[kept:])
    raised = jnp.zeros((1,), jnp.int32) if first else state[2]
    shape = pltpu.HBM((PADDED, 128), F32)
    if last:
        out_shape, out_specs = jax.ShapeDtypeStruct((16, 64, 128), BF16), vmem
    else:
        out_shape = (shape, shape, jax.ShapeDtypeStruct((1,), jnp.int32))
        out_specs = (HBM, HBM, smem)
    return pl.pallas_call(
        functools.partial(attend_kernel, groups=groups, first=first, last=last),
        out_shape=out_shape,
        in_specs=[smem] * 6 + [vmem] * 3 + [HBM] * (len(operands) - 3),
        out_specs=out_specs,
        input_output_aliases={} if first or last else {11: 0, 12: 1},
        scratch_shapes=[
            pltpu.VMEM((PADDED, 128), F32),
            pltpu.VMEM((PADDED, 128), F32),
            pltpu.VMEM((BLOCK, 128), BF16),
            pltpu.VMEM((BLOCK // 2, 128), BF16),
            pltpu.VMEM((PADDED, 128), BF16),
            pltpu.VMEM((2 * groups, PAIR, 128), BF16),
            pltpu.VMEM((2 * groups, 128, KEYS), BF16),
            pltpu.VMEM((2 * groups, KEYS, 128), BF16),
            pltpu.SMEM((1,), jnp.int32),
            pltpu.SemaphoreType.DMA,
            pltpu.SemaphoreType.DMA((2 * groups + 2,)),
        ],
        compiler_params=pltpu.CompilerParams(vmem_limit_bytes=44 << 20),
        name="attend",
    )(place, which, start, count, bias, raised, *operands)


def out_kernel(
    yl_ref, parts_ref, tokens_ref, gain_ref, shared, resid_ref, ffn_in_ref, rows_scr, weight_scr, sems
):
    loads = []
    for side in range(2):
        half = yl_ref[0] if side == 0 else 1 - yl_ref[0]
        for i in range(8):
            target = pl.ds(pl.multiple_of(half * 512 + i * 64, 64), 64)
            source = shared.at[i, pl.ds(UNITS + side * 64, 64)]
            loads.append(
                pltpu.make_async_copy(source, weight_scr.at[target], sems.at[side * 8 + i])
            )
    for load in loads:
        load.start()
    left = lax.broadcasted_iota(jnp.int32, (64, 128), 1) < HEAD_DIM
    for t in range(8):
        low, high = parts_ref[t].astype(F32), parts_ref[8 + t].astype(F32)
        at = slice(t * 128, (t + 1) * 128)
        rows_scr[:64, at] = jnp.where(left, low, pltpu.roll(high, 64, 1)).astype(BF16)
        rows_scr[64:, at] = jnp.where(left, pltpu.roll(low, 64, 1), high).astype(BF16)
    for load in loads:
        load.wait()
    resid = tokens_ref[...].astype(F32) + jnp.dot(
        rows_scr[...], weight_scr[...], preferred_element_type=F32
    )
    resid_ref[...] = resid
    ffn_in_ref[...] = norm_rows(resid, gain_ref[...]).astype(BF16)


def out_projection(yl, parts, tokens, gain, shared):
    vmem = pl.BlockSpec(memory_space=pltpu.VMEM)
    return pl.pallas_call(
        out_kernel,
        out_shape=(
            jax.ShapeDtypeStruct(tokens.shape, F32),
            jax.ShapeDtypeStruct(tokens.shape, BF16),
        ),
        in_specs=[pl.BlockSpec(memory_space=pltpu.SMEM)] + [vmem] * 3 + [HBM],
        out_specs=(vmem, vmem),
        scratch_shapes=[
            pltpu.VMEM(tokens.shape, BF16),
            pltpu.VMEM((1024, 1024), BF16),
            pltpu.SemaphoreType.DMA((16,)),
        ],
        name="out_projection",
    )(
        yl,
        parts,
        tokens,
        gain.reshape(1, -1),
        pltpu.with_memory_space_constraint(shared, pltpu.HBM),
    )


def ffn_kernel(rows_ref, shared, out_ref, rows_scr, shared_scr, sems):
    rows_load = pltpu.make_async_copy(rows_ref, rows_scr, sems.at[8])
    rows_load.start()
    copies = [
        pltpu.make_async_copy(shared.at[i, pl.ds(0, UNITS)], shared_scr.at[i], sems.at[i])
        for i in range(shared.shape[0])
    ]
    for copy in copies:
        copy.start()
    dot = functools.partial(jnp.dot, preferred_element_type=F32)
    rows_load.wait()
    x = rows_scr[...]
    total = None
    for low in range(0, len(copies), 2):
        copies[low].wait()
        copies[low + 1].wait()
        both = dot(x[:, :512], shared_scr[low, :512, :])
        both = both + dot(x[:, 512:], shared_scr[low + 1, :512, :])
        hidden = (jax.nn.silu(both[:, :512]) * both[:, 512:]).astype(BF16)
        part = dot(hidden[:, :256], shared_scr[low, 512:UNITS, :])
        part = part + dot(hidden[:, 256:], shared_scr[low + 1, 512:UNITS, :])
        total = part if total is None else total + part
    out_ref[...] = total.astype(out_ref.dtype)


def feed_forward(rows, shared, dtype):
    return pl.pallas_call(
        ffn_kernel,
        out_shape=jax.ShapeDtypeStruct(rows.shape, dtype),
        in_specs=[HBM, HBM],
        out_specs=pl.BlockSpec(memory_space=pltpu.VMEM),
        scratch_shapes=[
            pltpu.VMEM(rows.shape, BF16),
            pltpu.VMEM((8, UNITS, 1024), BF16),
            pltpu.SemaphoreType.DMA((9,)),
        ],
        compiler_params=pltpu.CompilerParams(vmem_limit_bytes=40 << 20),
        name="feed_forward",
    )(
        pltpu.with_memory_space_constraint(rows, pltpu.HBM),
        pltpu.with_memory_space_constraint(shared, pltpu.HBM),
    )


def per_device(
    tokens,
    segment_ids,
    variate_ids,
    time_ids,
    attn_gain,
    q_weight,
    k_weight,
    v_weight,
    out_weight,
    var_bias,
    ffn_gain,
    gate_weight,
    up_weight,
    down_weight,
):
    z, yh, c = lax.axis_index("z"), lax.axis_index("yh"), lax.axis_index("c")
    pick = functools.partial(lax.dynamic_index_in_dim, keepdims=False)

    swap = [(0, 1), (1, 0)]
    number = lambda *values: jnp.stack(values).astype(jnp.int32)
    lane = lax.broadcasted_iota(jnp.int32, (1, 128), 1)

    with jax.named_scope("gather_normed"):
        normed = norm_rows(tokens, attn_gain).astype(BF16)
        rows = gather_rows(normed, TP, 8)

    with jax.named_scope("tables"):
        freq = 10000.0 ** (-2.0 * (lane & 31).astype(F32) / HEAD_DIM)
        angle = time_ids.astype(F32)[:, None] * freq
        cosine, sine = jnp.cos(angle), jnp.sin(angle)
        bias = pick(var_bias, yh, 1)
        rest = rest_bias = (bias[0] - bias[1]) * LOG2E
        pieces = []
        for _ in range(3):
            piece = lax.reduce_precision(rest, 8, 7)
            pieces.append(piece)
            rest = rest - piece
        take = lax.dynamic_slice_in_dim
        segments = segment_ids.reshape(256, 128)
        variates = variate_ids.reshape(256, 128)
        at = number(z * 32 + c * 8, z * 32 + 16 + c * 8)
        extra = query_side(at, jnp.stack(pieces), variates, segments)
        blocks = segment_ids.reshape(8, 2, 2, BLOCK)
        q_seg = pick(pick(blocks, z, 0), c, 1).reshape(1, PAIR)
        low_seg = segments[::16, :1]
        high_seg = segments[15::16, 127:]
        begin = jnp.sum((q_seg < low_seg).astype(jnp.int32), axis=1)
        end = jnp.sum((q_seg <= high_seg).astype(jnp.int32), axis=1)
        start = begin // 64 * 64
        count = jnp.where(end > begin, (end - start + ROWS - 1) // ROWS, 0)
        out_own = take(out_weight, c * 64, 64)
        out_near = lax.ppermute(out_own, "yl", swap)
        pack = jnp.concatenate(
            [
                jnp.concatenate(
                    [take(gate_weight, c * 512, 512), take(up_weight, c * 512, 512)], axis=1
                ),
                take(down_weight, c * 256, 256),
                out_own,
                out_near,
            ],
            axis=0,
        )
        rows, cosine, sine, extra, start, count, pack = lax.optimization_barrier(
            (rows, cosine, sine, extra, start, count, pack)
        )

    with jax.named_scope("share_weights"):
        shared = lax.all_gather(pack, ("x", "c"), axis=0, tiled=True).reshape(8, UNITS + 128, 1024)

    with jax.named_scope("project"):
        mine, send, q_here = project(
            number(yh), rows, q_weight, k_weight, v_weight, cosine, sine
        )

    with jax.named_scope("exchange"):
        there = lax.ppermute(send, "yh", swap)
        mine = lax.dynamic_update_slice_in_dim(mine, there[:BLOCK], BLOCK, axis=0)

    with jax.named_scope("attention"):
        ahead = lambda array, k: lax.ppermute(array, "z", [(i, (i - k) % 8) for i in range(8)])
        place = number(yh, c)
        gap = rest_bias.reshape(1)
        state = None
        parts = [mine]
        hops = ((0,), (1, 7), (2, 6), (3, 5), (4,))
        for hop, steps in enumerate(hops):
            others = [lax.ppermute(part, "c", swap) for part in parts]
            which = number(
                *((z + k) % 8 * 2 + side for k in steps for side in (yh, 1 - yh))
            )
            coming = [ahead(parts[0], 1)] if hop < 4 else []
            if hop < 3:
                coming.append(ahead(parts[-1], -1))
            state = attend(
                place,
                which,
                start,
                count,
                gap,
                (q_here, there, extra),
                (variates, segments),
                [part for pair in zip(parts, others) for part in pair],
                state,
                hop == 4,
            )
            if hop < 4:
                state, parts = lax.optimization_barrier((state, coming))
        state, shared = lax.optimization_barrier((state, shared))

    with jax.named_scope("to_rows"):
        attended = lax.all_to_all(state, ("yh", "yl", "x"), 0, 0, tiled=True)

    with jax.named_scope("out_projection"):
        resid, ffn_in = out_projection(
            number(lax.axis_index("yl")), attended, tokens, ffn_gain, shared
        )

    with jax.named_scope("feed_forward"):
        away = lax.ppermute(ffn_in, "yl", swap)
        own = feed_forward(ffn_in, shared, F32)
        own, away = lax.optimization_barrier((own, away))
        far = feed_forward(away, shared, BF16)
        back = lax.ppermute(far, "yl", swap)
        return (resid + (own + back.astype(F32))).astype(BF16)


def solution(mesh):
    split = Mesh(mesh.devices.reshape(8, 2, 2, 2, 4), ("z", "yh", "c", "yl", "x"))
    return jax.shard_map(
        per_device,
        mesh=split,
        in_specs=(
            P(REQ + TP, None),
            P(),
            P(),
            P(REQ),
            P(),
            P(None, TP),
            P(None, TP),
            P(None, TP),
            P(TP, None),
            P(None, TP),
            P(),
            P(None, TP),
            P(None, TP),
            P(TP, None),
        ),
        out_specs=P(REQ + TP, None),
        check_vma=False,
    )
```
